256 devices in a mesh: section: 16 (over z, core), expert: 16 (over x, y).
Axes of the slice: x: 4, y: 4, z: 8, core: 2. Of those that a mesh axis runs over, the one named last changes fastest.
Arguments:
- left_in: bfloat16 [16, 1024, 2048], P('section', 'expert'), may hold values from -6 to 6
- left_new: bfloat16 [1024, 2048], P('expert'), may hold values from -6 to 6
- left_saved: bfloat16 [16, 1024, 2048], P('section', 'expert'), may hold values from -6 to 6
- left_cot: bfloat16 [16, 1024, 2048], P('section', 'expert'), may hold values from -6 to 6
- right_in: bfloat16 [16, 1024, 2048], P('section', 'expert'), may hold values from -6 to 6
- right_saved: bfloat16 [2, 16, 1024, 2048], P(None, 'section', 'expert'), may hold values from -6 to 6
- right_cot: bfloat16 [16, 1024, 2048], P('section', 'expert'), may hold values from -6 to 6
- right_cot_new: bfloat16 [1024, 2048], P('expert'), may hold values from -6 to 6
- expert_ids: int32 [3, 2, 16, 1024, 1], P(None, None, 'section', 'expert'), may hold values from 0 to 7; in each aligned block of 64 rows (0 to 63, 64 to 127, ..., all dimensions but the last counted through in order) at most 10 rows name the same one
- gate_values: float32 [3, 2, 16, 1024, 1], P(None, None, 'section', 'expert'), may hold values from 0.25 to 1
- w_gate: bfloat16 [16, 16, 2048, 384], P('section', 'expert'), may hold values from -0.125 to 0.125
- w_up: bfloat16 [16, 16, 2048, 384], P('section', 'expert'), may hold values from -0.125 to 0.125
- w_down: bfloat16 [16, 16, 384, 2048], P('section', 'expert'), may hold values from -0.21875 to 0.21875
Outputs:
- left_out: bfloat16 [2, 16, 1024, 2048], P(None, 'section', 'expert')
- right_out: bfloat16 [16, 1024, 2048], P('section', 'expert')
- left_back: bfloat16 [16, 1024, 2048], P('section', 'expert')
- right_back: bfloat16 [2, 16, 1024, 2048], P(None, 'section', 'expert')
- grad_gate: bfloat16 [16, 16, 2048, 384], P('section', 'expert')
- grad_up: bfloat16 [16, 16, 2048, 384], P('section', 'expert')
- grad_down: bfloat16 [16, 16, 384, 2048], P('section', 'expert')
The draws below stay inside these ranges and needn't reach their ends.
Inputs may be any that keep to these rules, and one draw needn't show every extreme that they name: `expert_ids`: each row names one expert. In each aligned block of 64 rows (one device's tokens in one pass) no expert is named by more than 10 rows, and in some blocks one expert is named by exactly 10 rows.
All inputs are finite; a program needn't handle non-finite values.
Results may differ from the reference program's by a relative error of at most 0.0064.
Values may be sent and summed in bfloat16 or wider, within the bound.
A program may use at most 128 MiB of HBM per device.

```python
import math
from functools import partial
import jax
import jax.numpy as jnp
import numpy as np
from jax import lax

D = 2048
FF = 768
TOP = 1
SLOTS = 3
TOK_DEV = 64
HALF = 384
EXPERTS = 8
CAP = 10
TOKENS = 1024
SECTIONS = 16
N_EXPERT = 16


def level_of(stream_key, dims, shards, smallest, top_value):
    def one(dim, blocks):
        heights = jax.random.uniform(jax.random.fold_in(jax.random.fold_in(stream_key, 6), dim), (blocks,), jnp.float32, smallest / len(shards), top_value / len(shards))
        return jnp.repeat(jnp.exp(heights), dims[dim] // blocks).reshape((-1,) + (1,) * (len(dims) - dim - 1))

    loudness = one(*shards[0])
    for cut in shards[1:]:
        loudness = loudness * one(*cut)
    return loudness


def deal_out(stream_key, own, number, rows, number_of, top, most, lean):
    sequence = jax.random.permutation(stream_key, number_of)
    heavy_load, usual = portions_of(number_of, rows * top, most, lean, True), portions_of(number_of, rows * top, most, lean, False)
    places = jnp.arange(number_of)

    def named(lengths, offset_by):
        used = int((lengths > 0).sum())
        fixed = max(1, used // 4)
        passed = fixed + (places - fixed + offset_by * (used - fixed)) % max(1, number_of - fixed)
        return jnp.zeros((number_of,), jnp.int32).at[sequence[jnp.where(places < fixed, places, passed)]].set(jnp.asarray(lengths, jnp.int32))

    lengths = jnp.where(number % 4 == 0, named(heavy_load, number // 4), named(usual, number - number // 4 - 1))
    mixed = jax.random.permutation(jax.random.fold_in(own, 3), number_of)
    source_of, receiver = mixed[0:number_of // 2 * 2:2], mixed[1:number_of // 2 * 2:2]
    slack = jnp.minimum(lengths[source_of] - 1, most - lengths[receiver]) // 2
    slack = jnp.where((source_of == sequence[0]) | (receiver == sequence[0]) | (lengths[receiver] == 0), 0, jnp.maximum(slack, 0))
    passed = jax.random.randint(jax.random.fold_in(own, 4), (number_of // 2,), 0, 1 << 20) % (slack + 1)
    lengths = lengths.at[source_of].add(-passed).at[receiver].add(passed)
    members = jnp.searchsorted(jnp.cumsum(lengths), jnp.arange(rows * top), side="right").astype(jnp.int32)
    table = members.reshape(top, rows).T
    table = table[jax.random.permutation(jax.random.fold_in(own, 1), rows)]
    offset_by = jax.random.randint(jax.random.fold_in(own, 2), (rows, 1), 0, top)
    return jnp.take_along_axis(table, (jnp.arange(top)[None, :] + offset_by) % top, axis=1)


def portions_of(amount, total, reach, lean, full):
    loads = [(1 << 20) // math.isqrt(standing ** lean) + 1 for standing in range(1, amount + 1)]
    largest = reach if full else min(reach, max(-(-total // amount), total * loads[0] // sum(loads)))
    least = 1 if total - largest >= amount - 1 else 0
    holding, spare = [largest] + [least] * (amount - 1), total - largest - least * (amount - 1)
    while spare > 0:
        movable = [i for i in range(1, amount) if holding[i] < largest] or [i for i in range(1, amount) if holding[i] < reach]
        mass, left = sum([loads[i] for i in movable]), spare
        for i in movable:
            more = min(reach - holding[i], max(1, left * loads[i] // mass), spare)
            holding[i] = holding[i] + more
            spare = spare - more
    return np.array(holding)


def noise(rng, dims, spread, most, split=(), held_as=jnp.bfloat16):
    entries = spread * jax.random.normal(rng, dims, jnp.float32)
    if split:
        entries = entries * level_of(rng, dims, split, -0.22, 0.18)
    return jnp.clip(entries, -most, most).astype(held_as)


def setup_inputs(seed: int = 0) -> dict:
    splits = jax.random.split(jax.random.key(seed), 14)
    left_in = noise(splits[0], (SECTIONS, TOKENS, D), 1.0, 6.0, ((0, 16), (1, 16)))
    left_new = noise(splits[1], (TOKENS, D), 1.0, 6.0, ((0, 16),))
    left_saved = noise(splits[2], (SECTIONS, TOKENS, D), 1.0, 6.0, ((0, 16), (1, 16)))
    left_cot = noise(splits[3], (SECTIONS, TOKENS, D), 1.0, 6.0, ((0, 16), (1, 16)))
    right_in = noise(splits[4], (SECTIONS, TOKENS, D), 1.0, 6.0, ((0, 16), (1, 16)))
    right_saved = noise(splits[5], (2, SECTIONS, TOKENS, D), 1.0, 6.0, ((1, 16), (2, 16)))
    right_cot = noise(splits[6], (SECTIONS, TOKENS, D), 1.0, 6.0, ((0, 16), (1, 16)))
    right_cot_new = noise(splits[7], (TOKENS, D), 1.0, 6.0, ((0, 16),))
    expert_ids_keys = jax.random.split(jax.random.fold_in(splits[8], 1), SLOTS * 2 * SECTIONS * TOKENS // TOK_DEV)
    expert_ids_turns = jax.random.permutation(jax.random.fold_in(splits[8], 3), SLOTS * 2 * SECTIONS * TOKENS // TOK_DEV)
    expert_ids = jax.vmap(lambda own, number: deal_out(jax.random.fold_in(splits[8], 2), own, number, TOK_DEV, EXPERTS, TOP, CAP, 2))(expert_ids_keys, expert_ids_turns).reshape((SLOTS, 2, SECTIONS, TOKENS, TOP))
    gate_values = jnp.clip(0.25 + 0.75 * jax.random.uniform(splits[9], (SLOTS, 2, SECTIONS, TOKENS, TOP), jnp.float32) ** level_of(splits[9], (SLOTS, 2, SECTIONS, TOKENS, TOP), ((2, 16), (3, 16)), -0.2, 0.2), 0.25, 1.0)
    w_gate = noise(splits[10], (SECTIONS, 2 * EXPERTS, D, HALF), D ** -0.5, 0.125, ((0, 16), (1, 16)))
    w_up = noise(splits[11], (SECTIONS, 2 * EXPERTS, D, HALF), D ** -0.5, 0.125, ((0, 16), (1, 16)))
    w_down = noise(splits[12], (SECTIONS, 2 * EXPERTS, HALF, D), FF ** -0.5, 0.21875, ((0, 16), (1, 16)))
    return {"left_in": left_in, "left_new": left_new, "left_saved": left_saved, "left_cot": left_cot, "right_in": right_in, "right_saved": right_saved, "right_cot": right_cot, "right_cot_new": right_cot_new, "expert_ids": expert_ids, "gate_values": gate_values, "w_gate": w_gate, "w_up": w_up, "w_down": w_down}


HIGHEST = lax.Precision.HIGHEST


def route_tables(ids_block, gates_block, experts, capacity):
    token_count = ids_block.shape[0]
    top_count = ids_block.shape[1]
    flat_ids = ids_block.reshape(-1).astype(jnp.int32)
    onehot = (flat_ids[:, None] == jnp.arange(experts, dtype=jnp.int32)[None, :]).astype(jnp.int32)
    before = jnp.cumsum(onehot, axis=0) - onehot
    position = jnp.sum(before * onehot, axis=1)
    target = (flat_ids * capacity + position).reshape(token_count, top_count)
    slot_ids = jnp.arange(experts * capacity, dtype=jnp.int32)
    matches = target[None, :, :] == slot_ids[:, None, None]
    placement = jnp.sum(matches.astype(jnp.float32), axis=2)
    weighting = jnp.sum(jnp.where(matches, gates_block[None, :, :], jnp.zeros_like(gates_block)[None]), axis=2)
    return placement, weighting


def expert_forward(expert_rows, gate_half, up_half, down_half):
    gate_act = jnp.dot(expert_rows, gate_half, preferred_element_type=jnp.float32)
    up_act = jnp.dot(expert_rows, up_half, preferred_element_type=jnp.float32)
    hidden = (gate_act * jax.nn.sigmoid(gate_act) * up_act).astype(jnp.bfloat16)
    return jnp.dot(hidden, down_half, preferred_element_type=jnp.float32)


def expert_backward(expert_rows, row_cot, gate_half, up_half, down_half):
    gate_act = jnp.dot(expert_rows, gate_half, preferred_element_type=jnp.float32)
    up_act = jnp.dot(expert_rows, up_half, preferred_element_type=jnp.float32)
    logistic = jax.nn.sigmoid(gate_act)
    swish = gate_act * logistic
    hidden = (swish * up_act).astype(jnp.bfloat16)
    d_hidden = jnp.dot(row_cot, down_half.T, preferred_element_type=jnp.float32)
    d_gate = (d_hidden * up_act * logistic * (1.0 + gate_act * (1.0 - logistic))).astype(jnp.bfloat16)
    d_up = (d_hidden * swish).astype(jnp.bfloat16)
    grad_down = jnp.dot(hidden.T, row_cot, preferred_element_type=jnp.float32)
    grad_gate = jnp.dot(expert_rows.T, d_gate, preferred_element_type=jnp.float32)
    grad_up = jnp.dot(expert_rows.T, d_up, preferred_element_type=jnp.float32)
    backward_rows = jnp.dot(d_gate, gate_half.T, preferred_element_type=jnp.float32) + jnp.dot(d_up, up_half.T, preferred_element_type=jnp.float32)
    return backward_rows, grad_gate, grad_up, grad_down


def add_halves(lower, upper):
    return (lower.astype(jnp.bfloat16).astype(jnp.float32) + upper.astype(jnp.bfloat16).astype(jnp.float32)).astype(jnp.bfloat16)


def to_experts(routed, experts, capacity):
    blocks = routed.shape[0]
    model_width = routed.shape[2]
    return routed.reshape(blocks, experts, capacity, model_width).transpose(1, 0, 2, 3).reshape(experts, blocks * capacity, model_width)


def to_blocks(routed, blocks, capacity):
    experts = routed.shape[0]
    model_width = routed.shape[2]
    return routed.reshape(experts, blocks, capacity, model_width).transpose(1, 0, 2, 3).reshape(blocks, experts * capacity, model_width)


def section_tables(ids_section, gates_section):
    experts = N_EXPERT // 2
    tables = jax.vmap(partial(route_tables, experts=experts, capacity=CAP))
    return tables(ids_section.reshape(N_EXPERT, TOK_DEV, TOP), gates_section.reshape(N_EXPERT, TOK_DEV, TOP))


def section_forward(operands):
    tokens, ids_section, gates_section, gate_pairs, up_pairs, down_pairs = operands
    experts = N_EXPERT // 2
    model_width = tokens.shape[1]
    token_blocks = tokens.reshape(N_EXPERT, TOK_DEV, model_width)
    placement, weighting = section_tables(ids_section, gates_section)
    routed = jnp.einsum("bst,btd->bsd", placement, token_blocks.astype(jnp.float32), precision=HIGHEST).astype(jnp.bfloat16)
    per_expert = to_experts(routed, experts, CAP)

    def one_expert(expert_operands):
        expert_rows, gate_pair, up_pair, down_pair = expert_operands
        lower = expert_forward(expert_rows, gate_pair[0], up_pair[0], down_pair[0])
        upper = expert_forward(expert_rows, gate_pair[1], up_pair[1], down_pair[1])
        return add_halves(lower, upper)

    outputs = lax.map(one_expert, (per_expert, gate_pairs.reshape(experts, 2, model_width, HALF), up_pairs.reshape(experts, 2, model_width, HALF), down_pairs.reshape(experts, 2, HALF, model_width)))
    by_block = to_blocks(outputs, N_EXPERT, CAP)
    mixed_out = token_blocks.astype(jnp.float32) + jnp.einsum("bst,bsd->btd", weighting, by_block.astype(jnp.float32), precision=HIGHEST)
    return mixed_out.reshape(tokens.shape).astype(jnp.bfloat16)


def section_backward(operands):
    tokens, cotangent, ids_section, gates_section, gate_pairs, up_pairs, down_pairs = operands
    experts = N_EXPERT // 2
    model_width = tokens.shape[1]
    token_blocks = tokens.reshape(N_EXPERT, TOK_DEV, model_width)
    cot_blocks = cotangent.reshape(N_EXPERT, TOK_DEV, model_width)
    placement, weighting = section_tables(ids_section, gates_section)
    routed = jnp.einsum("bst,btd->bsd", placement, token_blocks.astype(jnp.float32), precision=HIGHEST).astype(jnp.bfloat16)
    row_cot = jnp.einsum("bst,btd->bsd", weighting, cot_blocks.astype(jnp.float32), precision=HIGHEST).astype(jnp.bfloat16)

    def one_expert(expert_operands):
        expert_rows, expert_cot, gate_pair, up_pair, down_pair = expert_operands
        lower = expert_backward(expert_rows, expert_cot, gate_pair[0], up_pair[0], down_pair[0])
        upper = expert_backward(expert_rows, expert_cot, gate_pair[1], up_pair[1], down_pair[1])
        summed = add_halves(lower[0], upper[0])
        return summed, jnp.stack([lower[1], upper[1]]), jnp.stack([lower[2], upper[2]]), jnp.stack([lower[3], upper[3]])

    results = lax.map(one_expert, (to_experts(routed, experts, CAP), to_experts(row_cot, experts, CAP), gate_pairs.reshape(experts, 2, model_width, HALF), up_pairs.reshape(experts, 2, model_width, HALF), down_pairs.reshape(experts, 2, HALF, model_width)))
    by_block = to_blocks(results[0], N_EXPERT, CAP)
    new_cot = cot_blocks.astype(jnp.float32) + jnp.einsum("bst,bsd->btd", placement, by_block.astype(jnp.float32), precision=HIGHEST)
    grad_gate = results[1].reshape(2 * experts, model_width, HALF)
    grad_up = results[2].reshape(2 * experts, model_width, HALF)
    grad_down = results[3].reshape(2 * experts, HALF, model_width)
    return new_cot.reshape(cotangent.shape).astype(jnp.bfloat16), grad_gate, grad_up, grad_down


def backward_cot(operands):
    return section_backward(operands)[0]


def three_passes(operands):
    passes, section_weights = operands
    totals = []
    cots = []
    for saved_rows, cot_rows, ids_section, gates_section in passes:
        result = section_backward((saved_rows, cot_rows, ids_section, gates_section) + section_weights)
        cots.append(result[0])
        if len(totals) == 0:
            totals = [result[1], result[2], result[3]]
        else:
            totals = [totals[0] + result[1], totals[1] + result[2], totals[2] + result[3]]
    return cots[1], cots[2], totals[0].astype(jnp.bfloat16), totals[1].astype(jnp.bfloat16), totals[2].astype(jnp.bfloat16)


def reference(left_in, left_new, left_saved, left_cot, right_in, right_saved, right_cot, right_cot_new, expert_ids, gate_values, w_gate, w_up, w_down):
    saved_zero = right_saved[0][::-1]
    saved_two = right_saved[1][::-1]
    cot_zero = right_cot[::-1]
    left_zero = lax.map(section_forward, (left_in, expert_ids[0, 0], gate_values[0, 0], w_gate, w_up, w_down))
    back_zero = lax.map(backward_cot, (saved_zero, cot_zero, expert_ids[0, 1], gate_values[0, 1], w_gate, w_up, w_down))
    right_one = lax.map(section_forward, (right_in[::-1], expert_ids[1, 0], gate_values[1, 0], w_gate, w_up, w_down))
    left_two_in = jnp.concatenate([left_new[None], left_zero[:-1]], axis=0)
    left_two = lax.map(section_forward, (left_two_in, expert_ids[2, 0], gate_values[2, 0], w_gate, w_up, w_down))
    cot_two = jnp.concatenate([back_zero[1:], right_cot_new[None]], axis=0)
    passes = ((saved_zero, cot_zero, expert_ids[0, 1], gate_values[0, 1]), (left_saved, left_cot, expert_ids[1, 1], gate_values[1, 1]), (saved_two, cot_two, expert_ids[2, 1], gate_values[2, 1]))
    back_one, back_two, grad_gate, grad_up, grad_down = lax.map(three_passes, (passes, (w_gate, w_up, w_down)))
    left_out = jnp.stack([left_zero, left_two])
    right_back = jnp.stack([back_zero, back_two])
    return left_out, right_one, back_one, right_back, grad_gate, grad_up, grad_down
```

```python
import jax
import jax.numpy as jnp
from jax import lax
from jax.experimental import pallas as pl
from jax.experimental.pallas import tpu as pltpu
from jax.sharding import PartitionSpec as P

BF = jnp.bfloat16
F32 = jnp.float32
MESH = pl.DeviceIdType.MESH
TOK = 64
D = 2048
HALF = 384
SLAB = 2560
CHUNK = 512
ROWS = 160

F0, B0, F1, B1, F2, B2 = range(6)
U_F0, U_B1X, U_B1C, U_B0X, U_B0C, U_F1, U_B2X, U_F2, U_B2C = range(9)


def iota(shape, dim):
    return lax.broadcasted_iota(jnp.int32, shape, dim)


def dot(a, b):
    return jnp.dot(a, b, preferred_element_type=F32)


def dot_nt(a, b):
    return lax.dot_general(a, b, (((1,), (1,)), ((), ())), preferred_element_type=F32)


def dot_tn(a, b):
    return lax.dot_general(a, b, (((0,), (0,)), ((), ())), preferred_element_type=F32)


def kernel(
    ids_ref,
    gates_ref,
    left_in,
    left_new,
    left_saved,
    left_cot,
    right_in,
    right_saved,
    right_cot,
    right_cot_new,
    w_gate,
    w_up,
    w_down,
    left_out,
    right_out,
    left_back,
    right_back,
    grad_gate,
    grad_up,
    grad_down,
    ptab,
    pttab,
    gtab,
    wgu,
    wd,
    tok,
    mir,
    passed,
    outs,
    send,
    recv,
    part,
    half,
    sums,
    vals,
    xall,
    call,
    dgu,
    hid,
    xfwd,
    gg_buf,
    gu_buf,
    gd_buf,
    load_sem,
    mir_sem,
    s1_send,
    s1_recv,
    rl_send,
    rl_recv,
    pt_send,
    pt_recv,
    sm_send,
    sm_recv,
    ps_sem,
    out_sem,
):
    sec = lax.axis_index("section")
    me = lax.axis_index("expert")
    x = lax.div(me, 4)
    y = lax.rem(me, 4)
    pair = lax.div(y, 2)
    partner = x * 4 + (y + 1 - 2 * lax.rem(y, 2))
    mine = 2 * x + pair
    mirror = 15 - sec
    after = lax.rem(sec + 1, 16)
    ahead = lax.rem(sec + 15, 16)

    peers = []
    for step in (2, 1, 3, 0):
        xd = lax.rem(x + step, 4)
        for a in (1, 0):
            if step == 0 and a == 0:
                continue
            yd = 3 - y if a else y
            group = 1 - pair if a else pair
            peers.append((xd * 4 + yd, a, xd, 2 * xd + group))

    def local(src, dst, sem):
        return pltpu.make_async_copy(src, dst, sem)

    def remote(src, dst, ssem, rsem, section, expert):
        return pltpu.make_async_remote_copy(
            src_ref=src,
            dst_ref=dst,
            send_sem=ssem,
            recv_sem=rsem,
            device_id=(section, expert),
            device_id_type=MESH,
        )

    loads = [
        local(left_in.at[0], tok.at[0], load_sem.at[0]),
        local(left_saved.at[0], tok.at[1], load_sem.at[1]),
        local(left_cot.at[0], tok.at[2], load_sem.at[2]),
        local(w_gate.at[0, 0], wgu.at[:, pl.ds(0, HALF)], load_sem.at[3]),
        local(w_up.at[0, 0], wgu.at[:, pl.ds(HALF, HALF)], load_sem.at[4]),
        local(w_down.at[0, 0], wd, load_sem.at[5]),
        local(left_new, tok.at[3], load_sem.at[6]),
        local(right_cot_new, tok.at[4], load_sem.at[7]),
    ]
    for copy in loads:
        copy.start()

    barrier = pltpu.get_barrier_semaphore()
    for dest, _, _, _ in peers:
        pl.semaphore_signal(barrier, inc=1, device_id=(sec, dest), device_id_type=MESH)
    pl.semaphore_signal(barrier, inc=1, device_id=(sec, partner), device_id_type=MESH)
    for other in (mirror, after, ahead):
        pl.semaphore_signal(barrier, inc=1, device_id=(other, me), device_id_type=MESH)

    eye = iota((TOK, TOK), 0) == iota((TOK, TOK), 1)
    upper = (iota((TOK, TOK), 0) < iota((TOK, TOK), 1)).astype(BF)

    def code_of(j):
        q = j % 8
        return (lax.div(j, 8) % 8) * 16 + jnp.where(j < 64, q, 8 + lax.div(q, 4))

    code_rows = code_of(iota((128, TOK), 0)).astype(F32)
    code_cols = code_of(iota((TOK, 128), 1)).astype(F32)
    for p in range(6):
        ids = ids_ref[p : p + 1, :]
        onehot = (ids == iota((8, TOK), 0)).astype(F32)
        before = dot(onehot.astype(BF), upper)
        rank = jnp.sum(before * onehot, axis=0, keepdims=True)
        target = ids.astype(F32) * 16.0 + rank
        ptab[p] = (code_rows == target).astype(F32).astype(BF)
        column = jnp.sum(jnp.where(eye, target, 0.0), axis=1, keepdims=True)
        pttab[p] = (code_cols == column).astype(F32).astype(BF)
        gate = jnp.sum(jnp.where(eye, gates_ref[p : p + 1, :], 0.0), axis=1, keepdims=True)
        gtab[p] = jnp.broadcast_to(gate, (TOK, 128))

    pl.semaphore_wait(barrier, 11)

    mirror_sources = [right_cot.at[0], right_saved.at[0, 0], right_in.at[0], right_saved.at[1, 0]]
    mirrors = [
        remote(src, mir.at[i], mir_sem.at[0, i], mir_sem.at[1, i], mirror, me)
        for i, src in enumerate(mirror_sources)
    ]
    for copy in mirrors:
        copy.start()

    quarter64 = iota((TOK, CHUNK), 0) % 4
    quarter128 = iota((128, CHUNK), 0) % 4

    def gather(unit, p, read, scaled):
        place = ptab[p]
        extra = None
        for c in range(4):
            cols = pl.ds(c * CHUNK, CHUNK)
            block = read(cols)
            if scaled:
                block = (gtab[p][:, 0:1] * block.astype(F32)).astype(BF)
            routed = dot(place, block)
            send[unit, :, :, cols] = routed[:64].reshape(8, 8, CHUNK).astype(BF)
            tail = routed[64:]
            extra = tail if c == 0 else jnp.where(quarter64 == c, tail, extra)
        send[unit, :, :, pl.ds(D, CHUNK)] = extra.reshape(8, 8, CHUNK).astype(BF)
        for dest, a, _, expert in peers:
            remote(
                send.at[unit, expert],
                recv.at[unit, 4 * a + x],
                s1_send.at[unit],
                s1_recv.at[unit, a],
                sec,
                dest,
            ).start()
        recv[unit, x] = send[unit, mine]

    def relay(unit):
        for a in (1, 0):
            count = 4 if a else 3
            span = recv.at[unit, pl.ds(4 * a, count)]
            remote(span, span, s1_send.at[unit], s1_recv.at[unit, a], sec, partner).wait_recv()
            remote(
                recv.at[unit, pl.ds(4 * a, 4)],
                recv.at[unit, pl.ds(8 + 4 * a, 4)],
                rl_send.at[unit, a],
                rl_recv.at[unit, a],
                sec,
                partner,
            ).start()

    def relayed(unit):
        for a in (1, 0):
            span = recv.at[unit, pl.ds(4 * a, 4)]
            remote(span, span, rl_send.at[unit, a], rl_recv.at[unit, a], sec, partner).wait_recv()

    pick_j = iota((32, 128), 1)
    pick_r = iota((32, 128), 0)
    spread = (lax.div(iota((128, 32), 0), 4) == iota((128, 32), 1)).astype(F32).astype(BF)

    def unfold(unit, dst, base):
        for c in range(4):
            cols = pl.ds(c * CHUNK, CHUNK)
            first = recv[unit, :, :, cols].astype(F32).reshape(128, CHUNK).astype(BF)
            dst[pl.ds(base, 128), cols] = first
        tail = recv[unit, :, :, pl.ds(D, CHUNK)].astype(F32).reshape(128, CHUNK).astype(BF)
        for c in range(4):
            pick = (pick_j == 4 * pick_r + c).astype(F32).astype(BF)
            dst[pl.ds(base + 128, 32), pl.ds(c * CHUNK, CHUNK)] = dot(pick, tail).astype(BF)

    def fold(r, chunk_of):
        extra = None
        for c in range(4):
            rows = chunk_of(c)
            part[r, :, :, pl.ds(c * CHUNK, CHUNK)] = (
                rows[:128].reshape(16, 8, CHUNK).astype(BF)
            )
            tail = dot(spread, rows[128:].astype(BF))
            extra = tail if c == 0 else jnp.where(quarter128 == c, tail, extra)
        part[r, :, :, pl.ds(D, CHUNK)] = extra.reshape(16, 8, CHUNK).astype(BF)
        remote(
            part.at[r, pl.ds(8, 8)], half.at[r], pt_send.at[r], pt_recv.at[r], sec, partner
        ).start()

    def gate_up(rows):
        return [dot(rows[...], wgu[:, pl.ds(256 * i, 256)]) for i in range(3)]

    def expert_forward(unit, r):
        relayed(unit)
        unfold(unit, xfwd, 0)
        both = jnp.concatenate(gate_up(xfwd), axis=1)
        gate, up = both[:, :HALF], both[:, HALF:]
        hidden = (gate * jax.nn.sigmoid(gate) * up).astype(BF)
        fold(r, lambda c: dot(hidden, wd[:, pl.ds(c * CHUNK, CHUNK)]))

    def expert_backward(unit_x, unit_c, index, r):
        base = index * ROWS
        rows = pl.ds(base, ROWS)
        relayed(unit_x)
        unfold(unit_x, xall, base)
        both = jnp.concatenate(gate_up(xall.at[rows]), axis=1)
        gate, up = both[:, :HALF], both[:, HALF:]
        logistic = jax.nn.sigmoid(gate)
        swish = gate * logistic
        hid[rows] = (swish * up).astype(BF)
        relayed(unit_c)
        unfold(unit_c, call, base)
        d_hidden = dot_nt(call[rows], wd[...])
        d_gate = (d_hidden * up * logistic * (1.0 + gate * (1.0 - logistic))).astype(BF)
        d_up = (d_hidden * swish).astype(BF)
        dgu[rows, pl.ds(0, HALF)] = d_gate
        dgu[rows, pl.ds(HALF, HALF)] = d_up
        fold(r, lambda c: dot_nt(dgu[rows], wgu[pl.ds(c * CHUNK, CHUNK), :]))

    def add_halves(r):
        remote(half.at[r], half.at[r], pt_send.at[r], pt_recv.at[r], sec, partner).wait_recv()
        for i in range(8):
            sums[r, i] = (part[r, i].astype(F32) + half[r, i].astype(F32)).astype(BF)
        for dest, a, xd, _ in peers:
            remote(
                sums.at[r, 4 * a + xd],
                vals.at[r, mine],
                sm_send.at[r],
                sm_recv.at[r],
                sec,
                dest,
            ).start()
        vals[r, mine] = sums[r, x]

    def combine(r, p, read, scaled, index):
        span = vals.at[r, pl.ds(0, 7)]
        remote(span, span, sm_send.at[r], sm_recv.at[r], sec, partner).wait_recv()
        back = pttab[p]
        tail = vals[r, :, :, pl.ds(D, CHUNK)].astype(F32).reshape(TOK, CHUNK)
        for c in range(4):
            cols = pl.ds(c * CHUNK, CHUNK)
            first = vals[r, :, :, cols].astype(F32).reshape(TOK, CHUNK)
            last = jnp.where(quarter64 == c, tail, 0.0)
            rows = jnp.concatenate([first, last], axis=0).astype(BF)
            got = dot(back, rows)
            if scaled:
                got = gtab[p][:, 0:1] * got
            outs[index, :, cols] = (read(cols).astype(F32) + got).astype(BF)

    def from_tok(i):
        return lambda cols: tok[i, :, cols]

    def from_mir(i):
        return lambda cols: mir[i, :, cols]

    def choose(edge, i, j):
        return lambda cols: jnp.where(
            sec == edge, tok[i, :, cols].astype(F32), passed[j, :, cols].astype(F32)
        ).astype(BF)

    left_two = choose(0, 3, 0)
    cot_two = choose(15, 4, 1)
    pass_left = remote(outs.at[0], passed.at[0], ps_sem.at[0, 0], ps_sem.at[1, 0], after, me)
    pass_right = remote(outs.at[1], passed.at[1], ps_sem.at[0, 1], ps_sem.at[1, 1], ahead, me)
    out_copies = [
        local(outs.at[0], left_out.at[0], out_sem.at[0]),
        local(outs.at[1], right_back.at[0], out_sem.at[1]),
        local(outs.at[2], right_out, out_sem.at[2]),
        local(outs.at[3], left_back, out_sem.at[3]),
        local(outs.at[4], left_out.at[1], out_sem.at[4]),
        local(outs.at[5], right_back.at[1], out_sem.at[5]),
        local(gg_buf, grad_gate, out_sem.at[6]),
        local(gu_buf, grad_up, out_sem.at[7]),
        local(gd_buf, grad_down, out_sem.at[8]),
    ]

    R_F0, R_B0, R_F1, R_B1, R_F2, R_B2 = range(6)
    loads[0].wait()
    gather(U_F0, F0, from_tok(0), False)
    loads[1].wait()
    gather(U_B1X, B1, from_tok(1), False)
    loads[2].wait()
    relay(U_F0)
    gather(U_B1C, B1, from_tok(2), True)
    relay(U_B1X)
    relay(U_B1C)
    for copy in loads[3:]:
        copy.wait()
    expert_forward(U_F0, R_F0)
    mirrors[0].wait_recv()
    gather(U_B0C, B0, from_mir(0), True)
    mirrors[1].wait_recv()
    gather(U_B0X, B0, from_mir(1), False)
    relay(U_B0C)
    relay(U_B0X)
    expert_backward(U_B1X, U_B1C, 0, R_B1)
    add_halves(R_F0)
    combine(R_F0, F0, from_tok(0), True, 0)
    pass_left.start()
    out_copies[0].start()
    pass_left.wait_recv()
    gather(U_F2, F2, left_two, False)
    relay(U_F2)
    expert_backward(U_B0X, U_B0C, 1, R_B0)
    add_halves(R_B1)
    combine(R_B1, B1, from_tok(2), False, 3)
    out_copies[3].start()
    mirrors[2].wait_recv()
    gather(U_F1, F1, from_mir(2), False)
    mirrors[3].wait_recv()
    gather(U_B2X, B2, from_mir(3), False)
    relay(U_F1)
    relay(U_B2X)
    expert_forward(U_F2, R_F2)
    add_halves(R_B0)
    combine(R_B0, B0, from_mir(0), False, 1)
    pass_right.start()
    out_copies[1].start()
    pass_right.wait_recv()
    gather(U_B2C, B2, cot_two, True)
    relay(U_B2C)
    expert_forward(U_F1, R_F1)
    add_halves(R_F2)
    combine(R_F2, F2, left_two, True, 4)
    out_copies[4].start()
    expert_backward(U_B2X, U_B2C, 2, R_B2)
    add_halves(R_F1)
    combine(R_F1, F1, from_mir(2), True, 2)
    out_copies[2].start()

    def grads_of_inputs(i, carry):
        cols = pl.ds(pl.multiple_of(i * 256, 256), 256)
        total = dot_tn(xall[:, cols], dgu[...]).astype(BF)
        gg_buf[cols, :] = total[:, :HALF]
        gu_buf[cols, :] = total[:, HALF:]
        return carry

    def grads_of_down(i, carry):
        cols = pl.ds(pl.multiple_of(i * 256, 256), 256)
        gd_buf[:, cols] = dot_tn(hid[...], call[:, cols]).astype(BF)
        return carry

    lax.fori_loop(0, 8, grads_of_inputs, 0)
    out_copies[6].start()
    out_copies[7].start()
    add_halves(R_B2)
    lax.fori_loop(0, 8, grads_of_down, 0)
    out_copies[8].start()
    combine(R_B2, B2, cot_two, False, 5)
    out_copies[5].start()

    for copy in mirrors:
        copy.wait_send()
    pass_left.wait_send()
    pass_right.wait_send()
    for unit in range(9):
        span = send.at[unit, pl.ds(0, 7)]
        remote(span, span, s1_send.at[unit], s1_recv.at[unit, 0], sec, partner).wait_send()
        for a in range(2):
            span = recv.at[unit, pl.ds(4 * a, 4)]
            remote(span, span, rl_send.at[unit, a], rl_recv.at[unit, a], sec, partner).wait_send()
    for r in range(6):
        span = part.at[r, pl.ds(8, 8)]
        remote(span, span, pt_send.at[r], pt_recv.at[r], sec, partner).wait_send()
        span = sums.at[r, pl.ds(0, 7)]
        remote(span, span, sm_send.at[r], sm_recv.at[r], sec, partner).wait_send()
    for copy in out_copies:
        copy.wait()


def per_device(
    left_in,
    left_new,
    left_saved,
    left_cot,
    right_in,
    right_saved,
    right_cot,
    right_cot_new,
    expert_ids,
    gate_values,
    w_gate,
    w_up,
    w_down,
):
    ids = expert_ids.reshape(6, TOK)
    gates = gate_values.reshape(6, TOK)
    anywhere = pl.BlockSpec(memory_space=pl.ANY)
    vmem = pl.BlockSpec(memory_space=pltpu.VMEM)
    sds = jax.ShapeDtypeStruct
    dma = pltpu.SemaphoreType.DMA
    outs = pl.pallas_call(
        kernel,
        name="relay",
        out_shape=(
            sds((2, TOK, D), BF),
            sds((TOK, D), BF),
            sds((TOK, D), BF),
            sds((2, TOK, D), BF),
            sds((D, HALF), BF),
            sds((D, HALF), BF),
            sds((HALF, D), BF),
        ),
        in_specs=[vmem, vmem] + [anywhere] * 11,
        out_specs=(anywhere,) * 7,
        scratch_shapes=[
            pltpu.VMEM((6, 128, TOK), BF),
            pltpu.VMEM((6, TOK, 128), BF),
            pltpu.VMEM((6, TOK, 128), F32),
            pltpu.VMEM((D, 2 * HALF), BF),
            pltpu.VMEM((HALF, D), BF),
            pltpu.VMEM((5, TOK, D), BF),
            pltpu.VMEM((4, TOK, D), BF),
            pltpu.VMEM((2, TOK, D), BF),
            pltpu.VMEM((6, TOK, D), BF),
            pltpu.VMEM((9, 8, 8, SLAB), BF),
            pltpu.VMEM((9, 16, 8, SLAB), BF),
            pltpu.VMEM((6, 16, 8, SLAB), BF),
            pltpu.VMEM((6, 8, 8, SLAB), BF),
            pltpu.VMEM((6, 8, 8, SLAB), BF),
            pltpu.VMEM((6, 8, 8, SLAB), BF),
            pltpu.VMEM((3 * ROWS, D), BF),
            pltpu.VMEM((3 * ROWS, D), BF),
            pltpu.VMEM((3 * ROWS, 2 * HALF), BF),
            pltpu.VMEM((3 * ROWS, HALF), BF),
            pltpu.VMEM((ROWS, D), BF),
            pltpu.VMEM((D, HALF), BF),
            pltpu.VMEM((D, HALF), BF),
            pltpu.VMEM((HALF, D), BF),
            dma((8,)),
            dma((2, 4)),
            dma((9,)),
            dma((9, 2)),
            dma((9, 2)),
            dma((9, 2)),
            dma((6,)),
            dma((6,)),
            dma((6,)),
            dma((6,)),
            dma((2, 2)),
            dma((9,)),
        ],
        compiler_params=pltpu.CompilerParams(
            collective_id=0, has_side_effects=True, vmem_limit_bytes=62 * 1024 * 1024
        ),
    )(
        ids,
        gates,
        left_in,
        left_new,
        left_saved,
        left_cot,
        right_in,
        right_saved,
        right_cot,
        right_cot_new,
        w_gate,
        w_up,
        w_down,
    )
    left_out, right_out, left_back, right_back, gg, gu, gd = outs
    return (
        left_out[:, None],
        right_out[None],
        left_back[None],
        right_back[:, None],
        gg[None, None],
        gu[None, None],
        gd[None, None],
    )


def solution(mesh):
    in_specs = (
        P("section", "expert", None),
        P("expert", None),
        P("section", "expert", None),
        P("section", "expert", None),
        P("section", "expert", None),
        P(None, "section", "expert", None),
        P("section", "expert", None),
        P("expert", None),
        P(None, None, "section", "expert", None),
        P(None, None, "section", "expert", None),
        P("section", "expert", None, None),
        P("section", "expert", None, None),
        P("section", "expert", None, None),
    )
    out_specs = (
        P(None, "section", "expert", None),
        P("section", "expert", None),
        P("section", "expert", None),
        P(None, "section", "expert", None),
        P("section", "expert", None, None),
        P("section", "expert", None, None),
        P("section", "expert", None, None),
    )
    return jax.shard_map(
        per_device, mesh=mesh, in_specs=in_specs, out_specs=out_specs, check_vma=False
    )
```

```python
import jax
import jax.numpy as jnp
from jax import lax
from jax.experimental import pallas as pl
from jax.experimental.pallas import tpu as pltpu
from jax.sharding import PartitionSpec as P

BF = jnp.bfloat16
F32 = jnp.float32
MESH = pl.DeviceIdType.MESH
TOK = 64
D = 2048
HALF = 384
SLAB = 2560
CHUNK = 512
ROWS = 160

F0, B0, F1, B1, F2, B2 = range(6)
U_F0, U_B1X, U_B1C, U_B0X, U_B0C, U_F1, U_B2X, U_F2, U_B2C = range(9)


def iota(shape, dim):
    return lax.broadcasted_iota(jnp.int32, shape, dim)


def dot(a, b):
    return jnp.dot(a, b, preferred_element_type=F32)


def dot_nt(a, b):
    return lax.dot_general(a, b, (((1,), (1,)), ((), ())), preferred_element_type=F32)


def dot_tn(a, b):
    return lax.dot_general(a, b, (((0,), (0,)), ((), ())), preferred_element_type=F32)


def kernel(
    ids_hbm,
    gates_hbm,
    left_in,
    left_new,
    left_saved,
    left_cot,
    right_in,
    right_saved,
    right_cot,
    right_cot_new,
    w_gate,
    w_up,
    w_down,
    outs,
    gg_buf,
    gu_buf,
    gd_buf,
    ids_ref,
    gates_ref,
    ptab,
    pttab,
    gtab,
    wgu,
    wd,
    tok,
    mir,
    passed,
    send,
    recv,
    part,
    half,
    sums,
    vals,
    xall,
    call,
    dgu,
    hid,
    xfwd,
    load_sem,
    mir_sem,
    s1_send,
    s1_recv,
    rl_send,
    rl_recv,
    pt_send,
    pt_recv,
    sm_send,
    sm_recv,
    ps_sem,
):
    sec = lax.axis_index("section")
    me = lax.axis_index("expert")
    x = lax.div(me, 4)
    y = lax.rem(me, 4)
    pair = lax.div(y, 2)
    partner = x * 4 + (y + 1 - 2 * lax.rem(y, 2))
    mine = 2 * x + pair
    mirror = 15 - sec
    after = lax.rem(sec + 1, 16)
    ahead = lax.rem(sec + 15, 16)

    peers = []
    for step in (2, 1, 3, 0):
        xd = lax.rem(x + step, 4)
        for a in (1, 0):
            if step == 0 and a == 0:
                continue
            yd = 3 - y if a else y
            group = 1 - pair if a else pair
            peers.append((xd * 4 + yd, a, xd, 2 * xd + group))

    def local(src, dst, sem):
        return pltpu.make_async_copy(src, dst, sem)

    def remote(src, dst, ssem, rsem, section, expert):
        return pltpu.make_async_remote_copy(
            src_ref=src,
            dst_ref=dst,
            send_sem=ssem,
            recv_sem=rsem,
            device_id=(section, expert),
            device_id_type=MESH,
        )

    id_loads = [
        local(ids_hbm, ids_ref, load_sem.at[8]),
        local(gates_hbm, gates_ref, load_sem.at[9]),
    ]
    loads = [
        local(left_in.at[0], tok.at[0], load_sem.at[0]),
        local(left_saved.at[0], tok.at[1], load_sem.at[1]),
        local(left_cot.at[0], tok.at[2], load_sem.at[2]),
        local(w_gate.at[0, 0], wgu.at[:, pl.ds(0, HALF)], load_sem.at[3]),
        local(w_up.at[0, 0], wgu.at[:, pl.ds(HALF, HALF)], load_sem.at[4]),
        local(w_down.at[0, 0], wd, load_sem.at[5]),
        local(left_new, tok.at[3], load_sem.at[6]),
        local(right_cot_new, tok.at[4], load_sem.at[7]),
    ]
    for copy in id_loads + loads:
        copy.start()

    barrier = pltpu.get_barrier_semaphore()
    for dest, _, _, _ in peers:
        pl.semaphore_signal(barrier, inc=1, device_id=(sec, dest), device_id_type=MESH)
    pl.semaphore_signal(barrier, inc=1, device_id=(sec, partner), device_id_type=MESH)
    for other in (mirror, after, ahead):
        pl.semaphore_signal(barrier, inc=1, device_id=(other, me), device_id_type=MESH)

    eye = iota((TOK, TOK), 0) == iota((TOK, TOK), 1)
    upper = (iota((TOK, TOK), 0) < iota((TOK, TOK), 1)).astype(BF)

    def code_of(j):
        q = j % 8
        return (lax.div(j, 8) % 8) * 16 + jnp.where(j < 64, q, 8 + lax.div(q, 4))

    code_rows = code_of(iota((128, TOK), 0)).astype(F32)
    code_cols = code_of(iota((TOK, 128), 1)).astype(F32)
    for copy in id_loads:
        copy.wait()
    for p in range(6):
        ids = ids_ref[p // 2, p % 2, 0]
        onehot = (ids == iota((8, TOK), 0)).astype(F32)
        before = dot(onehot.astype(BF), upper)
        rank = jnp.sum(before * onehot, axis=0, keepdims=True)
        target = ids.astype(F32) * 16.0 + rank
        ptab[p] = (code_rows == target).astype(F32).astype(BF)
        column = jnp.sum(jnp.where(eye, target, 0.0), axis=1, keepdims=True)
        pttab[p] = (code_cols == column).astype(F32).astype(BF)
        gate = jnp.sum(jnp.where(eye, gates_ref[p // 2, p % 2, 0], 0.0), axis=1, keepdims=True)
        gtab[p] = jnp.broadcast_to(gate, (TOK, 128))

    mirror_sources = [right_cot.at[0], right_saved.at[0, 0], right_in.at[0], right_saved.at[1, 0]]
    mirrors = [
        remote(src, mir.at[i], mir_sem.at[0, i], mir_sem.at[1, i], mirror, me)
        for i, src in enumerate(mirror_sources)
    ]

    quarter64 = iota((TOK, CHUNK), 0) % 4
    quarter128 = iota((128, CHUNK), 0) % 4

    def gather(unit, p, read, scaled):
        place = ptab[p]
        extra = None
        for c in range(4):
            cols = pl.ds(c * CHUNK, CHUNK)
            block = read(cols)
            if scaled:
                block = (gtab[p][:, 0:1] * block.astype(F32)).astype(BF)
            routed = dot(place, block)
            send[unit, :, :, cols] = routed[:64].reshape(8, 8, CHUNK).astype(BF)
            tail = routed[64:]
            extra = tail if c == 0 else jnp.where(quarter64 == c, tail, extra)
        send[unit, :, :, pl.ds(D, CHUNK)] = extra.reshape(8, 8, CHUNK).astype(BF)
        recv[unit, x] = send[unit, mine]

    def ship(unit):
        for dest, a, _, expert in peers:
            remote(
                send.at[unit, expert],
                recv.at[unit, 4 * a + x],
                s1_send.at[unit],
                s1_recv.at[unit, a],
                sec,
                dest,
            ).start()

    def relay(unit):
        for a in (1, 0):
            count = 4 if a else 3
            span = recv.at[unit, pl.ds(4 * a, count)]
            remote(span, span, s1_send.at[unit], s1_recv.at[unit, a], sec, partner).wait_recv()
            remote(
                recv.at[unit, pl.ds(4 * a, 4)],
                recv.at[unit, pl.ds(8 + 4 * a, 4)],
                rl_send.at[unit, a],
                rl_recv.at[unit, a],
                sec,
                partner,
            ).start()

    def relayed(unit):
        for a in (1, 0):
            span = recv.at[unit, pl.ds(4 * a, 4)]
            remote(span, span, rl_send.at[unit, a], rl_recv.at[unit, a], sec, partner).wait_recv()

    pick_j = iota((32, 128), 1)
    pick_r = iota((32, 128), 0)
    spread = (lax.div(iota((128, 32), 0), 4) == iota((128, 32), 1)).astype(F32).astype(BF)

    def unfold(unit, dst, base):
        for c in range(4):
            cols = pl.ds(c * CHUNK, CHUNK)
            first = recv[unit, :, :, cols].astype(F32).reshape(128, CHUNK).astype(BF)
            dst[pl.ds(base, 128), cols] = first
        tail = recv[unit, :, :, pl.ds(D, CHUNK)].astype(F32).reshape(128, CHUNK).astype(BF)
        for c in range(4):
            pick = (pick_j == 4 * pick_r + c).astype(F32).astype(BF)
            dst[pl.ds(base + 128, 32), pl.ds(c * CHUNK, CHUNK)] = dot(pick, tail).astype(BF)

    def fold(r, chunk_of):
        extra = None
        for c in range(4):
            rows = chunk_of(c)
            part[r, :, :, pl.ds(c * CHUNK, CHUNK)] = (
                rows[:128].reshape(16, 8, CHUNK).astype(BF)
            )
            tail = dot(spread, rows[128:].astype(BF))
            extra = tail if c == 0 else jnp.where(quarter128 == c, tail, extra)
        part[r, :, :, pl.ds(D, CHUNK)] = extra.reshape(16, 8, CHUNK).astype(BF)
        remote(
            part.at[r, pl.ds(8, 8)], half.at[r], pt_send.at[r], pt_recv.at[r], sec, partner
        ).start()

    def gate_up(rows):
        return [dot(rows[...], wgu[:, pl.ds(256 * i, 256)]) for i in range(3)]

    def expert_forward(unit, r):
        relayed(unit)
        unfold(unit, xfwd, 0)
        both = jnp.concatenate(gate_up(xfwd), axis=1)
        gate, up = both[:, :HALF], both[:, HALF:]
        hidden = (gate * jax.nn.sigmoid(gate) * up).astype(BF)
        fold(r, lambda c: dot(hidden, wd[:, pl.ds(c * CHUNK, CHUNK)]))

    def expert_backward(unit_x, unit_c, index, r):
        base = index * ROWS
        rows = pl.ds(base, ROWS)
        relayed(unit_x)
        unfold(unit_x, xall, base)
        both = jnp.concatenate(gate_up(xall.at[rows]), axis=1)
        gate, up = both[:, :HALF], both[:, HALF:]
        logistic = jax.nn.sigmoid(gate)
        swish = gate * logistic
        hid[rows] = (swish * up).astype(BF)
        relayed(unit_c)
        unfold(unit_c, call, base)
        d_hidden = dot_nt(call[rows], wd[...])
        d_gate = (d_hidden * up * logistic * (1.0 + gate * (1.0 - logistic))).astype(BF)
        d_up = (d_hidden * swish).astype(BF)
        dgu[rows, pl.ds(0, HALF)] = d_gate
        dgu[rows, pl.ds(HALF, HALF)] = d_up
        fold(r, lambda c: dot_nt(dgu[rows], wgu[pl.ds(c * CHUNK, CHUNK), :]))

    def add_halves(r):
        remote(half.at[r], half.at[r], pt_send.at[r], pt_recv.at[r], sec, partner).wait_recv()
        for i in range(8):
            sums[r, i] = (part[r, i].astype(F32) + half[r, i].astype(F32)).astype(BF)
        for dest, a, xd, _ in peers:
            remote(
                sums.at[r, 4 * a + xd],
                vals.at[r, mine],
                sm_send.at[r],
                sm_recv.at[r],
                sec,
                dest,
            ).start()
        vals[r, mine] = sums[r, x]

    def combine(r, p, read, scaled, index):
        span = vals.at[r, pl.ds(0, 7)]
        remote(span, span, sm_send.at[r], sm_recv.at[r], sec, partner).wait_recv()
        back = pttab[p]
        tail = vals[r, :, :, pl.ds(D, CHUNK)].astype(F32).reshape(TOK, CHUNK)
        for c in range(4):
            cols = pl.ds(c * CHUNK, CHUNK)
            first = vals[r, :, :, cols].astype(F32).reshape(TOK, CHUNK)
            last = jnp.where(quarter64 == c, tail, 0.0)
            rows = jnp.concatenate([first, last], axis=0).astype(BF)
            got = dot(back, rows)
            if scaled:
                got = gtab[p][:, 0:1] * got
            outs[index, :, cols] = (read(cols).astype(F32) + got).astype(BF)

    def from_tok(i):
        return lambda cols: tok[i, :, cols]

    def from_mir(i):
        return lambda cols: mir[i, :, cols]

    def choose(edge, i, j):
        return lambda cols: jnp.where(
            sec == edge, tok[i, :, cols].astype(F32), passed[j, :, cols].astype(F32)
        ).astype(BF)

    left_two = choose(0, 3, 0)
    cot_two = choose(15, 4, 1)
    pass_left = remote(outs.at[0], passed.at[0], ps_sem.at[0, 0], ps_sem.at[1, 0], after, me)
    pass_right = remote(outs.at[1], passed.at[1], ps_sem.at[0, 1], ps_sem.at[1, 1], ahead, me)
    R_F0, R_B0, R_F1, R_B1, R_F2, R_B2 = range(6)
    loads[0].wait()
    gather(U_F0, F0, from_tok(0), False)
    loads[1].wait()
    gather(U_B1X, B1, from_tok(1), False)
    loads[2].wait()
    gather(U_B1C, B1, from_tok(2), True)

    pl.semaphore_wait(barrier, 11)
    for copy in mirrors:
        copy.start()
    ship(U_F0)
    ship(U_B1X)
    ship(U_B1C)
    relay(U_F0)
    relay(U_B1X)
    relay(U_B1C)
    for copy in loads[3:]:
        copy.wait()
    expert_forward(U_F0, R_F0)
    mirrors[0].wait_recv()
    gather(U_B0C, B0, from_mir(0), True)
    ship(U_B0C)
    mirrors[1].wait_recv()
    gather(U_B0X, B0, from_mir(1), False)
    ship(U_B0X)
    relay(U_B0C)
    relay(U_B0X)
    expert_backward(U_B1X, U_B1C, 0, R_B1)
    add_halves(R_F0)
    combine(R_F0, F0, from_tok(0), True, 0)
    pass_left.start()
    pass_left.wait_recv()
    gather(U_F2, F2, left_two, False)
    ship(U_F2)
    relay(U_F2)
    expert_backward(U_B0X, U_B0C, 1, R_B0)
    add_halves(R_B1)
    combine(R_B1, B1, from_tok(2), False, 3)
    mirrors[2].wait_recv()
    gather(U_F1, F1, from_mir(2), False)
    ship(U_F1)
    mirrors[3].wait_recv()
    gather(U_B2X, B2, from_mir(3), False)
    ship(U_B2X)
    relay(U_F1)
    relay(U_B2X)
    expert_forward(U_F2, R_F2)
    add_halves(R_B0)
    combine(R_B0, B0, from_mir(0), False, 1)
    pass_right.start()
    pass_right.wait_recv()
    gather(U_B2C, B2, cot_two, True)
    ship(U_B2C)
    relay(U_B2C)
    expert_forward(U_F1, R_F1)
    add_halves(R_F2)
    combine(R_F2, F2, left_two, True, 4)
    expert_backward(U_B2X, U_B2C, 2, R_B2)
    add_halves(R_F1)
    combine(R_F1, F1, from_mir(2), True, 2)

    def grads_of_inputs(i, carry):
        cols = pl.ds(pl.multiple_of(i * 256, 256), 256)
        total = dot_tn(xall[:, cols], dgu[...]).astype(BF)
        gg_buf[cols, :] = total[:, :HALF]
        gu_buf[cols, :] = total[:, HALF:]
        return carry

    def grads_of_down(i, carry):
        cols = pl.ds(pl.multiple_of(i * 256, 256), 256)
        gd_buf[:, cols] = dot_tn(hid[...], call[:, cols]).astype(BF)
        return carry

    lax.fori_loop(0, 8, grads_of_inputs, 0)
    add_halves(R_B2)
    lax.fori_loop(0, 8, grads_of_down, 0)
    combine(R_B2, B2, cot_two, False, 5)

    for copy in mirrors:
        copy.wait_send()
    pass_left.wait_send()
    pass_right.wait_send()
    for unit in range(9):
        span = send.at[unit, pl.ds(0, 7)]
        remote(span, span, s1_send.at[unit], s1_recv.at[unit, 0], sec, partner).wait_send()
        for a in range(2):
            span = recv.at[unit, pl.ds(4 * a, 4)]
            remote(span, span, rl_send.at[unit, a], rl_recv.at[unit, a], sec, partner).wait_send()
    for r in range(6):
        span = part.at[r, pl.ds(8, 8)]
        remote(span, span, pt_send.at[r], pt_recv.at[r], sec, partner).wait_send()
        span = sums.at[r, pl.ds(0, 7)]
        remote(span, span, sm_send.at[r], sm_recv.at[r], sec, partner).wait_send()


def write_out(
    outs,
    gg_buf,
    gu_buf,
    gd_buf,
    left_out,
    right_out,
    left_back,
    right_back,
    grad_gate,
    grad_up,
    grad_down,
    sem,
):
    pairs = [
        (gg_buf, grad_gate),
        (gu_buf, grad_up),
        (gd_buf, grad_down),
        (outs.at[0], left_out.at[0]),
        (outs.at[1], right_back.at[0]),
        (outs.at[2], right_out),
        (outs.at[3], left_back),
        (outs.at[4], left_out.at[1]),
        (outs.at[5], right_back.at[1]),
    ]
    copies = [pltpu.make_async_copy(a, b, sem.at[i]) for i, (a, b) in enumerate(pairs)]
    for copy in copies:
        copy.start()
    for copy in copies:
        copy.wait()


def per_device(
    left_in,
    left_new,
    left_saved,
    left_cot,
    right_in,
    right_saved,
    right_cot,
    right_cot_new,
    expert_ids,
    gate_values,
    w_gate,
    w_up,
    w_down,
):
    ids = jnp.swapaxes(expert_ids, 3, 4)
    gates = jnp.swapaxes(gate_values, 3, 4)
    hbm = pl.BlockSpec(memory_space=pltpu.HBM)
    vmem = pl.BlockSpec(memory_space=pltpu.VMEM)
    sds = jax.ShapeDtypeStruct
    dma = pltpu.SemaphoreType.DMA
    results = pl.pallas_call(
        kernel,
        name="relay",
        out_shape=(
            pltpu.VMEM((6, TOK, D), BF),
            pltpu.VMEM((D, HALF), BF),
            pltpu.VMEM((D, HALF), BF),
            pltpu.VMEM((HALF, D), BF),
        ),
        in_specs=[hbm] * 13,
        out_specs=(vmem,) * 4,
        scratch_shapes=[
            pltpu.VMEM((3, 2, 1, 1, TOK), jnp.int32),
            pltpu.VMEM((3, 2, 1, 1, TOK), F32),
            pltpu.VMEM((6, 128, TOK), BF),
            pltpu.VMEM((6, TOK, 128), BF),
            pltpu.VMEM((6, TOK, 128), F32),
            pltpu.VMEM((D, 2 * HALF), BF),
            pltpu.VMEM((HALF, D), BF),
            pltpu.VMEM((5, TOK, D), BF),
            pltpu.VMEM((4, TOK, D), BF),
            pltpu.VMEM((2, TOK, D), BF),
            pltpu.VMEM((9, 8, 8, SLAB), BF),
            pltpu.VMEM((9, 16, 8, SLAB), BF),
            pltpu.VMEM((6, 16, 8, SLAB), BF),
            pltpu.VMEM((6, 8, 8, SLAB), BF),
            pltpu.VMEM((6, 8, 8, SLAB), BF),
            pltpu.VMEM((6, 8, 8, SLAB), BF),
            pltpu.VMEM((3 * ROWS, D), BF),
            pltpu.VMEM((3 * ROWS, D), BF),
            pltpu.VMEM((3 * ROWS, 2 * HALF), BF),
            pltpu.VMEM((3 * ROWS, HALF), BF),
            pltpu.VMEM((ROWS, D), BF),
            dma((10,)),
            dma((2, 4)),
            dma((9,)),
            dma((9, 2)),
            dma((9, 2)),
            dma((9, 2)),
            dma((6,)),
            dma((6,)),
            dma((6,)),
            dma((6,)),
            dma((2, 2)),
        ],
        compiler_params=pltpu.CompilerParams(
            collective_id=0, has_side_effects=True, vmem_limit_bytes=60700000
        ),
    )(
        ids,
        gates,
        left_in,
        left_new,
        left_saved,
        left_cot,
        right_in,
        right_saved,
        right_cot,
        right_cot_new,
        w_gate,
        w_up,
        w_down,
    )
    left_out, right_out, left_back, right_back, gg, gu, gd = pl.pallas_call(
        write_out,
        name="write_out",
        out_shape=(
            sds((2, TOK, D), BF),
            sds((TOK, D), BF),
            sds((TOK, D), BF),
            sds((2, TOK, D), BF),
            sds((D, HALF), BF),
            sds((D, HALF), BF),
            sds((HALF, D), BF),
        ),
        in_specs=[vmem] * 4,
        out_specs=(hbm,) * 7,
        scratch_shapes=[dma((9,))],
        compiler_params=pltpu.CompilerParams(vmem_limit_bytes=4 * 1024 * 1024),
    )(*results)
    return (
        left_out[:, None],
        right_out[None],
        left_back[None],
        right_back[:, None],
        gg[None, None],
        gu[None, None],
        gd[None, None],
    )


def solution(mesh):
    in_specs = (
        P("section", "expert", None),
        P("expert", None),
        P("section", "expert", None),
        P("section", "expert", None),
        P("section", "expert", None),
        P(None, "section", "expert", None),
        P("section", "expert", None),
        P("expert", None),
        P(None, None, "section", "expert", None),
        P(None, None, "section", "expert", None),
        P("section", "expert", None, None),
        P("section", "expert", None, None),
        P("section", "expert", None, None),
    )
    out_specs = (
        P(None, "section", "expert", None),
        P("section", "expert", None),
        P("section", "expert", None),
        P(None, "section", "expert", None),
        P("section", "expert", None, None),
        P("section", "expert", None, None),
        P("section", "expert", None, None),
    )
    return jax.shard_map(
        per_device, mesh=mesh, in_specs=in_specs, out_specs=out_specs, check_vma=False
    )
```

```python
import jax
import jax.numpy as jnp
from jax import lax
from jax.experimental import pallas as pl
from jax.experimental.pallas import tpu as pltpu
from jax.sharding import PartitionSpec as P

BF = jnp.bfloat16
F32 = jnp.float32
MESH = pl.DeviceIdType.MESH
TOK = 64
D = 2048
HALF = 384
SLAB = 2560
CHUNK = 512
ROWS = 160

F0, B0, F1, B1, F2, B2 = range(6)
U_F0, U_B1X, U_B1C, U_B0X, U_B0C, U_F1, U_B2X, U_F2, U_B2C = range(9)


def iota(shape, dim):
    return lax.broadcasted_iota(jnp.int32, shape, dim)


def dot(a, b):
    return jnp.dot(a, b, preferred_element_type=F32)


def dot_nt(a, b):
    return lax.dot_general(a, b, (((1,), (1,)), ((), ())), preferred_element_type=F32)


def dot_tn(a, b):
    return lax.dot_general(a, b, (((0,), (0,)), ((), ())), preferred_element_type=F32)


def kernel(
    ids_hbm,
    gates_hbm,
    left_in,
    left_new,
    left_saved,
    left_cot,
    right_in,
    right_saved,
    right_cot,
    right_cot_new,
    w_gate,
    w_up,
    w_down,
    outs,
    gg_buf,
    gu_buf,
    gd_buf,
    ids_ref,
    gates_ref,
    partner_ids,
    gathered,
    swapped,
    ptab,
    pttab,
    gtab,
    wgu,
    wd,
    tok,
    mir,
    passed,
    send,
    recv,
    part,
    half,
    sums,
    vals,
    xall,
    call,
    dgu,
    hid,
    xfwd,
    load_sem,
    mir_sem,
    s1_send,
    s1_recv,
    rl_send,
    rl_recv,
    pt_send,
    pt_recv,
    sm_send,
    sm_recv,
    ps_sem,
    id_sem,
    gt_sem,
):
    sec = lax.axis_index("section")
    me = lax.axis_index("expert")
    x = lax.div(me, 4)
    y = lax.rem(me, 4)
    pair = lax.div(y, 2)
    partner = x * 4 + (y + 1 - 2 * lax.rem(y, 2))
    mine = 2 * x + pair
    mirror = 15 - sec
    after = lax.rem(sec + 1, 16)
    ahead = lax.rem(sec + 15, 16)

    peers = []
    for step in (2, 1, 3, 0):
        xd = lax.rem(x + step, 4)
        for a in (1, 0):
            if step == 0 and a == 0:
                continue
            yd = 3 - y if a else y
            group = 1 - pair if a else pair
            peers.append((xd * 4 + yd, a, xd, 2 * xd + group))

    def local(src, dst, sem):
        return pltpu.make_async_copy(src, dst, sem)

    def remote(src, dst, ssem, rsem, section, expert):
        return pltpu.make_async_remote_copy(
            src_ref=src,
            dst_ref=dst,
            send_sem=ssem,
            recv_sem=rsem,
            device_id=(section, expert),
            device_id_type=MESH,
        )

    id_loads = [
        local(ids_hbm, ids_ref, load_sem.at[8]),
        local(gates_hbm, gates_ref, load_sem.at[9]),
    ]
    loads = [
        local(left_in.at[0], tok.at[0], load_sem.at[0]),
        local(left_saved.at[0], tok.at[1], load_sem.at[1]),
        local(left_cot.at[0], tok.at[2], load_sem.at[2]),
        local(w_gate.at[0, 0], wgu.at[:, pl.ds(0, HALF)], load_sem.at[3]),
        local(w_up.at[0, 0], wgu.at[:, pl.ds(HALF, HALF)], load_sem.at[4]),
        local(w_down.at[0, 0], wd, load_sem.at[5]),
        local(left_new, tok.at[3], load_sem.at[6]),
        local(right_cot_new, tok.at[4], load_sem.at[7]),
    ]
    for copy in id_loads + loads:
        copy.start()

    barrier = pltpu.get_barrier_semaphore()
    for dest, _, _, _ in peers:
        pl.semaphore_signal(barrier, inc=1, device_id=(sec, dest), device_id_type=MESH)
    pl.semaphore_signal(barrier, inc=1, device_id=(sec, partner), device_id_type=MESH)
    for other in (mirror, after, ahead):
        pl.semaphore_signal(barrier, inc=1, device_id=(other, me), device_id_type=MESH)

    eye = iota((TOK, TOK), 0) == iota((TOK, TOK), 1)
    upper = (iota((TOK, TOK), 0) < iota((TOK, TOK), 1)).astype(BF)

    def code_of(j):
        q = j % 8
        return (lax.div(j, 8) % 8) * 16 + jnp.where(j < 64, q, 8 + lax.div(q, 4))

    code_rows = code_of(iota((128, TOK), 0)).astype(F32)
    code_cols = code_of(iota((TOK, 128), 1)).astype(F32)
    for copy in id_loads:
        copy.wait()

    def targets(ids):
        onehot = (ids == iota((8, TOK), 0)).astype(F32)
        before = dot(onehot.astype(BF), upper)
        rank = jnp.sum(before * onehot, axis=0, keepdims=True)
        return ids.astype(F32) * 16.0 + rank

    def way_back(target):
        column = jnp.sum(jnp.where(eye, target, 0.0), axis=1, keepdims=True)
        return (code_cols == column).astype(F32).astype(BF)

    for p in range(6):
        target = targets(ids_ref[p // 2, p % 2, 0])
        ptab[p] = (code_rows == target).astype(F32).astype(BF)
        pttab[p] = way_back(target)
        gate = jnp.sum(jnp.where(eye, gates_ref[p // 2, p % 2, 0], 0.0), axis=1, keepdims=True)
        gtab[p] = jnp.broadcast_to(gate, (TOK, 128))

    mirror_sources = [right_cot.at[0], right_saved.at[0, 0], right_in.at[0], right_saved.at[1, 0]]
    id_swap = remote(ids_ref, partner_ids, id_sem.at[0], id_sem.at[1], sec, partner)
    mirrors = [
        remote(src, mir.at[i], mir_sem.at[0, i], mir_sem.at[1, i], mirror, me)
        for i, src in enumerate(mirror_sources)
    ]

    quarter64 = iota((TOK, CHUNK), 0) % 4
    quarter128 = iota((128, CHUNK), 0) % 4

    def gather(unit, p, read, scaled):
        place = ptab[p]
        extra = None
        for c in range(4):
            cols = pl.ds(c * CHUNK, CHUNK)
            block = read(cols)
            if scaled:
                block = (gtab[p][:, 0:1] * block.astype(F32)).astype(BF)
            routed = dot(place, block)
            send[unit, :, :, cols] = routed[:64].reshape(8, 8, CHUNK).astype(BF)
            tail = routed[64:]
            extra = tail if c == 0 else jnp.where(quarter64 == c, tail, extra)
        send[unit, :, :, pl.ds(D, CHUNK)] = extra.reshape(8, 8, CHUNK).astype(BF)
        recv[unit, x] = send[unit, mine]

    def ship(unit):
        for dest, a, _, expert in peers:
            remote(
                send.at[unit, expert],
                recv.at[unit, 4 * a + x],
                s1_send.at[unit],
                s1_recv.at[unit, a],
                sec,
                dest,
            ).start()

    def relay(unit):
        for a in (1, 0):
            count = 4 if a else 3
            span = recv.at[unit, pl.ds(4 * a, count)]
            remote(span, span, s1_send.at[unit], s1_recv.at[unit, a], sec, partner).wait_recv()
            remote(
                recv.at[unit, pl.ds(4 * a, 4)],
                recv.at[unit, pl.ds(8 + 4 * a, 4)],
                rl_send.at[unit, a],
                rl_recv.at[unit, a],
                sec,
                partner,
            ).start()

    def relayed(unit):
        for a in (1, 0):
            span = recv.at[unit, pl.ds(4 * a, 4)]
            remote(span, span, rl_send.at[unit, a], rl_recv.at[unit, a], sec, partner).wait_recv()

    pick_j = iota((32, 128), 1)
    pick_r = iota((32, 128), 0)
    spread = (lax.div(iota((128, 32), 0), 4) == iota((128, 32), 1)).astype(F32).astype(BF)

    def unfold(unit, dst, base):
        for c in range(4):
            cols = pl.ds(c * CHUNK, CHUNK)
            first = recv[unit, :, :, cols].astype(F32).reshape(128, CHUNK).astype(BF)
            dst[pl.ds(base, 128), cols] = first
        tail = recv[unit, :, :, pl.ds(D, CHUNK)].astype(F32).reshape(128, CHUNK).astype(BF)
        for c in range(4):
            pick = (pick_j == 4 * pick_r + c).astype(F32).astype(BF)
            dst[pl.ds(base + 128, 32), pl.ds(c * CHUNK, CHUNK)] = dot(pick, tail).astype(BF)

    def fold(r, chunk_of):
        extra = None
        for c in range(4):
            rows = chunk_of(c)
            part[r, :, :, pl.ds(c * CHUNK, CHUNK)] = (
                rows[:128].reshape(16, 8, CHUNK).astype(BF)
            )
            tail = dot(spread, rows[128:].astype(BF))
            extra = tail if c == 0 else jnp.where(quarter128 == c, tail, extra)
        part[r, :, :, pl.ds(D, CHUNK)] = extra.reshape(16, 8, CHUNK).astype(BF)

    def hand_over(r):
        for a in (1, 0):
            remote(
                part.at[r, pl.ds(8 + 4 * a, 4)],
                half.at[r, pl.ds(4 * a, 4)],
                pt_send.at[r, a],
                pt_recv.at[r, a],
                sec,
                partner,
            ).start()

    def hand_out(r):
        for dest, a, xd, _ in peers:
            remote(
                part.at[r, 8 + 4 * a + xd],
                half.at[r, mine],
                pt_send.at[r, 0],
                pt_recv.at[r, 0],
                sec,
                dest,
            ).start()
        for dest, a, xd, _ in peers:
            remote(
                part.at[r, 4 * a + xd],
                vals.at[r, mine],
                sm_send.at[r],
                sm_recv.at[r],
                sec,
                dest,
            ).start()
        half[r, mine] = part[r, 8 + x]
        vals[r, mine] = part[r, x]

    def gate_up(rows):
        return [dot(rows[...], wgu[:, pl.ds(256 * i, 256)]) for i in range(3)]

    def expert_forward(unit, r, give):
        relayed(unit)
        unfold(unit, xfwd, 0)
        both = jnp.concatenate(gate_up(xfwd), axis=1)
        gate, up = both[:, :HALF], both[:, HALF:]
        hidden = (gate * jax.nn.sigmoid(gate) * up).astype(BF)
        fold(r, lambda c: dot(hidden, wd[:, pl.ds(c * CHUNK, CHUNK)]))
        give(r)

    def expert_backward(unit_x, unit_c, index, r):
        base = index * ROWS
        rows = pl.ds(base, ROWS)
        relayed(unit_x)
        unfold(unit_x, xall, base)
        both = jnp.concatenate(gate_up(xall.at[rows]), axis=1)
        gate, up = both[:, :HALF], both[:, HALF:]
        logistic = jax.nn.sigmoid(gate)
        swish = gate * logistic
        hid[rows] = (swish * up).astype(BF)
        relayed(unit_c)
        unfold(unit_c, call, base)
        d_hidden = dot_nt(call[rows], wd[...])
        d_gate = (d_hidden * up * logistic * (1.0 + gate * (1.0 - logistic))).astype(BF)
        d_up = (d_hidden * swish).astype(BF)
        dgu[rows, pl.ds(0, HALF)] = d_gate
        dgu[rows, pl.ds(HALF, HALF)] = d_up
        fold(r, lambda c: dot_nt(dgu[rows], wgu[pl.ds(c * CHUNK, CHUNK), :]))
        hand_over(r)

    def add_halves(r):
        for a in (1, 0):
            span = half.at[r, pl.ds(4 * a, 4)]
            remote(span, span, pt_send.at[r, a], pt_recv.at[r, a], sec, partner).wait_recv()
            for i in range(4 * a, 4 * a + 4):
                sums[r, i] = (part[r, i].astype(F32) + half[r, i].astype(F32)).astype(BF)
            for dest, side, xd, _ in peers:
                if side == a:
                    remote(
                        sums.at[r, 4 * a + xd],
                        vals.at[r, mine],
                        sm_send.at[r],
                        sm_recv.at[r],
                        sec,
                        dest,
                    ).start()
        vals[r, mine] = sums[r, x]

    def rows_back(slabs, back, c):
        first = slabs[:, :, pl.ds(c * CHUNK, CHUNK)].astype(F32).reshape(TOK, CHUNK)
        tail = slabs[:, :, pl.ds(D, CHUNK)].astype(F32).reshape(TOK, CHUNK)
        last = jnp.where(quarter64 == c, tail, 0.0)
        return dot(back, jnp.concatenate([first, last], axis=0).astype(BF))

    def arrived(r):
        span = vals.at[r, pl.ds(0, 7)]
        remote(span, span, sm_send.at[r], sm_recv.at[r], sec, partner).wait_recv()

    def combine(r, p, read, scaled, index):
        arrived(r)
        for c in range(4):
            cols = pl.ds(c * CHUNK, CHUNK)
            got = rows_back(vals.at[r], pttab[p], c)
            if scaled:
                got = gtab[p][:, 0:1] * got
            outs[index, :, cols] = (read(cols).astype(F32) + got).astype(BF)

    swap = remote(gathered, swapped, gt_sem.at[0], gt_sem.at[1], sec, partner)

    def swap_parts(r, p):
        id_swap.wait_recv()
        back = way_back(targets(partner_ids[p // 2, p % 2, 0]))
        span = half.at[r, pl.ds(0, 7)]
        remote(span, span, pt_send.at[r, 0], pt_recv.at[r, 0], sec, partner).wait_recv()
        for c in range(4):
            gathered[:, pl.ds(c * CHUNK, CHUNK)] = rows_back(half.at[r], back, c).astype(BF)
        swap.start()

    def combine_swapped(r, p, read, index):
        arrived(r)
        swap.wait_recv()
        for c in range(4):
            cols = pl.ds(c * CHUNK, CHUNK)
            both = rows_back(vals.at[r], pttab[p], c) + swapped[:, cols].astype(F32)
            got = gtab[p][:, 0:1] * both.astype(BF).astype(F32)
            outs[index, :, cols] = (read(cols).astype(F32) + got).astype(BF)

    def from_tok(i):
        return lambda cols: tok[i, :, cols]

    def from_mir(i):
        return lambda cols: mir[i, :, cols]

    def choose(edge, i, j):
        return lambda cols: jnp.where(
            sec == edge, tok[i, :, cols].astype(F32), passed[j, :, cols].astype(F32)
        ).astype(BF)

    left_two = choose(0, 3, 0)
    cot_two = choose(15, 4, 1)
    pass_left = remote(outs.at[0], passed.at[0], ps_sem.at[0, 0], ps_sem.at[1, 0], after, me)
    pass_right = remote(outs.at[1], passed.at[1], ps_sem.at[0, 1], ps_sem.at[1, 1], ahead, me)
    def grads_of_inputs(i, carry):
        cols = pl.ds(pl.multiple_of(i * 256, 256), 256)
        total = dot_tn(xall[:, cols], dgu[...]).astype(BF)
        gg_buf[cols, :] = total[:, :HALF]
        gu_buf[cols, :] = total[:, HALF:]
        return carry

    def grads_of_down(i, carry):
        cols = pl.ds(pl.multiple_of(i * 256, 256), 256)
        gd_buf[:, cols] = dot_tn(hid[...], call[:, cols]).astype(BF)
        return carry

    R_F0, R_B0, R_F1, R_B1, R_F2, R_B2 = range(6)
    loads[0].wait()
    gather(U_F0, F0, from_tok(0), False)
    loads[1].wait()
    gather(U_B1X, B1, from_tok(1), False)
    loads[2].wait()
    gather(U_B1C, B1, from_tok(2), True)

    pl.semaphore_wait(barrier, 11)
    for i in (0, 1, 2, 3):
        mirrors[i].start()
    id_swap.start()
    ship(U_B1X)
    ship(U_B1C)
    relay(U_B1X)
    ship(U_F0)
    relay(U_F0)
    relay(U_B1C)
    for copy in loads[3:]:
        copy.wait()
    expert_forward(U_F0, R_F0, hand_over)
    mirrors[0].wait_recv()
    gather(U_B0C, B0, from_mir(0), True)
    ship(U_B0C)
    mirrors[1].wait_recv()
    relay(U_B0C)
    gather(U_B0X, B0, from_mir(1), False)
    ship(U_B0X)
    relay(U_B0X)
    add_halves(R_F0)
    expert_backward(U_B1X, U_B1C, 0, R_B1)
    combine(R_F0, F0, from_tok(0), True, 0)
    pass_left.start()
    pass_left.wait_recv()
    gather(U_F2, F2, left_two, False)
    ship(U_F2)
    relay(U_F2)
    mirrors[2].wait_recv()
    add_halves(R_B1)
    gather(U_F1, F1, from_mir(2), False)
    ship(U_F1)
    mirrors[3].wait_recv()
    expert_backward(U_B0X, U_B0C, 1, R_B0)
    gather(U_B2X, B2, from_mir(3), False)
    ship(U_B2X)
    combine(R_B1, B1, from_tok(2), False, 3)
    relay(U_F1)
    expert_forward(U_F2, R_F2, hand_over)
    add_halves(R_B0)
    combine(R_B0, B0, from_mir(0), False, 1)
    pass_right.start()
    pass_right.wait_recv()
    gather(U_B2C, B2, cot_two, True)
    ship(U_B2C)
    relay(U_B2X)
    expert_forward(U_F1, R_F1, hand_out)
    relay(U_B2C)
    swap_parts(R_F1, F1)
    add_halves(R_F2)
    combine(R_F2, F2, left_two, True, 4)
    expert_backward(U_B2X, U_B2C, 2, R_B2)
    lax.fori_loop(0, 8, grads_of_inputs, 0)
    add_halves(R_B2)
    lax.fori_loop(0, 8, grads_of_down, 0)
    combine_swapped(R_F1, F1, from_mir(2), 2)
    combine(R_B2, B2, cot_two, False, 5)

    for copy in mirrors:
        copy.wait_send()
    id_swap.wait_send()
    swap.wait_send()
    pass_left.wait_send()
    pass_right.wait_send()
    for unit in range(9):
        span = send.at[unit, pl.ds(0, 7)]
        remote(span, span, s1_send.at[unit], s1_recv.at[unit, 0], sec, partner).wait_send()
        for a in range(2):
            span = recv.at[unit, pl.ds(4 * a, 4)]
            remote(span, span, rl_send.at[unit, a], rl_recv.at[unit, a], sec, partner).wait_send()
    for r in range(6):
        for a in range(1 if r == R_F1 else 2):
            span = part.at[r, pl.ds(8, 7 if r == R_F1 else 4)]
            remote(span, span, pt_send.at[r, a], pt_recv.at[r, a], sec, partner).wait_send()
        span = sums.at[r, pl.ds(0, 7)]
        remote(span, span, sm_send.at[r], sm_recv.at[r], sec, partner).wait_send()


def write_out(
    outs,
    gg_buf,
    gu_buf,
    gd_buf,
    left_out,
    right_out,
    left_back,
    right_back,
    grad_gate,
    grad_up,
    grad_down,
    sem,
):
    pairs = [
        (gg_buf, grad_gate),
        (gu_buf, grad_up),
        (gd_buf, grad_down),
        (outs.at[0], left_out.at[0]),
        (outs.at[1], right_back.at[0]),
        (outs.at[2], right_out),
        (outs.at[3], left_back),
        (outs.at[4], left_out.at[1]),
        (outs.at[5], right_back.at[1]),
    ]
    copies = [pltpu.make_async_copy(a, b, sem.at[i]) for i, (a, b) in enumerate(pairs)]
    for copy in copies:
        copy.start()
    for copy in copies:
        copy.wait()


def per_device(
    left_in,
    left_new,
    left_saved,
    left_cot,
    right_in,
    right_saved,
    right_cot,
    right_cot_new,
    expert_ids,
    gate_values,
    w_gate,
    w_up,
    w_down,
):
    ids = jnp.swapaxes(expert_ids, 3, 4)
    gates = jnp.swapaxes(gate_values, 3, 4)
    hbm = pl.BlockSpec(memory_space=pltpu.HBM)
    vmem = pl.BlockSpec(memory_space=pltpu.VMEM)
    sds = jax.ShapeDtypeStruct
    dma = pltpu.SemaphoreType.DMA
    results = pl.pallas_call(
        kernel,
        name="relay",
        out_shape=(
            pltpu.VMEM((6, TOK, D), BF),
            pltpu.VMEM((D, HALF), BF),
            pltpu.VMEM((D, HALF), BF),
            pltpu.VMEM((HALF, D), BF),
        ),
        in_specs=[hbm] * 13,
        out_specs=(vmem,) * 4,
        scratch_shapes=[
            pltpu.VMEM((3, 2, 1, 1, TOK), jnp.int32),
            pltpu.VMEM((3, 2, 1, 1, TOK), F32),
            pltpu.VMEM((3, 2, 1, 1, TOK), jnp.int32),
            pltpu.VMEM((TOK, D), BF),
            pltpu.VMEM((TOK, D), BF),
            pltpu.VMEM((6, 128, TOK), BF),
            pltpu.VMEM((6, TOK, 128), BF),
            pltpu.VMEM((6, TOK, 128), F32),
            pltpu.VMEM((D, 2 * HALF), BF),
            pltpu.VMEM((HALF, D), BF),
            pltpu.VMEM((5, TOK, D), BF),
            pltpu.VMEM((4, TOK, D), BF),
            pltpu.VMEM((2, TOK, D), BF),
            pltpu.VMEM((9, 8, 8, SLAB), BF),
            pltpu.VMEM((9, 16, 8, SLAB), BF),
            pltpu.VMEM((6, 16, 8, SLAB), BF),
            pltpu.VMEM((6, 8, 8, SLAB), BF),
            pltpu.VMEM((6, 8, 8, SLAB), BF),
            pltpu.VMEM((6, 8, 8, SLAB), BF),
            pltpu.VMEM((3 * ROWS, D), BF),
            pltpu.VMEM((3 * ROWS, D), BF),
            pltpu.VMEM((3 * ROWS, 2 * HALF), BF),
            pltpu.VMEM((3 * ROWS, HALF), BF),
            pltpu.VMEM((ROWS, D), BF),
            dma((10,)),
            dma((2, 4)),
            dma((9,)),
            dma((9, 2)),
            dma((9, 2)),
            dma((9, 2)),
            dma((6, 2)),
            dma((6, 2)),
            dma((6,)),
            dma((6,)),
            dma((2, 2)),
            dma((2,)),
            dma((2,)),
        ],
        compiler_params=pltpu.CompilerParams(
            collective_id=0, has_side_effects=True, vmem_limit_bytes=60700000
        ),
    )(
        ids,
        gates,
        left_in,
        left_new,
        left_saved,
        left_cot,
        right_in,
        right_saved,
        right_cot,
        right_cot_new,
        w_gate,
        w_up,
        w_down,
    )
    left_out, right_out, left_back, right_back, gg, gu, gd = pl.pallas_call(
        write_out,
        name="write_out",
        out_shape=(
            sds((2, TOK, D), BF),
            sds((TOK, D), BF),
            sds((TOK, D), BF),
            sds((2, TOK, D), BF),
            sds((D, HALF), BF),
            sds((D, HALF), BF),
            sds((HALF, D), BF),
        ),
        in_specs=[vmem] * 4,
        out_specs=(hbm,) * 7,
        scratch_shapes=[dma((9,))],
        compiler_params=pltpu.CompilerParams(vmem_limit_bytes=4 * 1024 * 1024),
    )(*results)
    return (
        left_out[:, None],
        right_out[None],
        left_back[None],
        right_back[:, None],
        gg[None, None],
        gu[None, None],
        gd[None, None],
    )


def solution(mesh):
    in_specs = (
        P("section", "expert", None),
        P("expert", None),
        P("section", "expert", None),
        P("section", "expert", None),
        P("section", "expert", None),
        P(None, "section", "expert", None),
        P("section", "expert", None),
        P("expert", None),
        P(None, None, "section", "expert", None),
        P(None, None, "section", "expert", None),
        P("section", "expert", None, None),
        P("section", "expert", None, None),
        P("section", "expert", None, None),
    )
    out_specs = (
        P(None, "section", "expert", None),
        P("section", "expert", None),
        P("section", "expert", None),
        P(None, "section", "expert", None),
        P("section", "expert", None, None),
        P("section", "expert", None, None),
        P("section", "expert", None, None),
    )
    return jax.shard_map(
        per_device, mesh=mesh, in_specs=in_specs, out_specs=out_specs, check_vma=False
    )
```

```python
import jax
import jax.numpy as jnp
from jax import lax
from jax.experimental import pallas as pl
from jax.experimental.pallas import tpu as pltpu
from jax.sharding import PartitionSpec as P

BF = jnp.bfloat16
F32 = jnp.float32
MESH = pl.DeviceIdType.MESH
TOK = 64
D = 2048
HALF = 384
SLAB = 2560
CHUNK = 512
ROWS = 160

F0, B0, F1, B1, F2, B2 = range(6)
U_F0, U_B1X, U_B1C, U_B0X, U_B0C, U_F1, U_B2X, U_F2, U_B2C = range(9)


def iota(shape, dim):
    return lax.broadcasted_iota(jnp.int32, shape, dim)


def dot(a, b):
    return jnp.dot(a, b, preferred_element_type=F32)


def dot_nt(a, b):
    return lax.dot_general(a, b, (((1,), (1,)), ((), ())), preferred_element_type=F32)


def dot_tn(a, b):
    return lax.dot_general(a, b, (((0,), (0,)), ((), ())), preferred_element_type=F32)


def kernel(
    ids_hbm,
    gates_hbm,
    left_in,
    left_new,
    left_saved,
    left_cot,
    right_in,
    right_saved,
    right_cot,
    right_cot_new,
    w_gate,
    w_up,
    w_down,
    outs,
    gg_buf,
    gu_buf,
    gd_buf,
    ids_ref,
    gates_ref,
    partner_ids,
    gathered,
    swapped,
    ptab,
    pttab,
    gtab,
    wgu,
    wd,
    tok,
    mir,
    passed,
    send,
    recv,
    part,
    half,
    sums,
    vals,
    xall,
    call,
    dgu,
    hid,
    xfwd,
    load_sem,
    mir_sem,
    s1_send,
    s1_recv,
    rl_send,
    rl_recv,
    pt_send,
    pt_recv,
    sm_send,
    sm_recv,
    ps_sem,
    id_sem,
    gt_sem,
):
    sec = lax.axis_index("section")
    me = lax.axis_index("expert")
    x = lax.div(me, 4)
    y = lax.rem(me, 4)
    pair = lax.div(y, 2)
    partner = x * 4 + (y + 1 - 2 * lax.rem(y, 2))
    mine = 2 * x + pair
    mirror = 15 - sec
    after = lax.rem(sec + 1, 16)
    ahead = lax.rem(sec + 15, 16)

    peers = []
    for step in (2, 1, 3, 0):
        xd = lax.rem(x + step, 4)
        for a in (1, 0):
            if step == 0 and a == 0:
                continue
            yd = 3 - y if a else y
            group = 1 - pair if a else pair
            peers.append((xd * 4 + yd, a, xd, 2 * xd + group))

    def local(src, dst, sem):
        return pltpu.make_async_copy(src, dst, sem)

    def remote(src, dst, ssem, rsem, section, expert):
        return pltpu.make_async_remote_copy(
            src_ref=src,
            dst_ref=dst,
            send_sem=ssem,
            recv_sem=rsem,
            device_id=(section, expert),
            device_id_type=MESH,
        )

    id_loads = [
        local(ids_hbm, ids_ref, load_sem.at[8]),
        local(gates_hbm, gates_ref, load_sem.at[9]),
    ]
    loads = [
        local(left_in.at[0], tok.at[0], load_sem.at[0]),
        local(left_saved.at[0], tok.at[1], load_sem.at[1]),
        local(left_cot.at[0], tok.at[2], load_sem.at[2]),
        local(w_gate.at[0, 0], wgu.at[:, pl.ds(0, HALF)], load_sem.at[3]),
        local(w_up.at[0, 0], wgu.at[:, pl.ds(HALF, HALF)], load_sem.at[4]),
        local(w_down.at[0, 0], wd, load_sem.at[5]),
        local(left_new, tok.at[3], load_sem.at[6]),
        local(right_cot_new, tok.at[4], load_sem.at[7]),
    ]
    for copy in id_loads + loads:
        copy.start()

    barrier = pltpu.get_barrier_semaphore()
    for dest, _, _, _ in peers:
        pl.semaphore_signal(barrier, inc=1, device_id=(sec, dest), device_id_type=MESH)
    pl.semaphore_signal(barrier, inc=1, device_id=(sec, partner), device_id_type=MESH)
    for other in (mirror, after, ahead):
        pl.semaphore_signal(barrier, inc=1, device_id=(other, me), device_id_type=MESH)

    eye = iota((TOK, TOK), 0) == iota((TOK, TOK), 1)
    upper = (iota((TOK, TOK), 0) < iota((TOK, TOK), 1)).astype(BF)

    def code_of(j):
        q = j % 8
        return (lax.div(j, 8) % 8) * 16 + jnp.where(j < 64, q, 8 + lax.div(q, 4))

    code_rows = code_of(iota((128, TOK), 0)).astype(F32)
    code_cols = code_of(iota((TOK, 128), 1)).astype(F32)
    for copy in id_loads:
        copy.wait()

    def targets(ids):
        onehot = (ids == iota((8, TOK), 0)).astype(F32)
        before = dot(onehot.astype(BF), upper)
        rank = jnp.sum(before * onehot, axis=0, keepdims=True)
        return ids.astype(F32) * 16.0 + rank

    def way_back(target):
        column = jnp.sum(jnp.where(eye, target, 0.0), axis=1, keepdims=True)
        return (code_cols == column).astype(F32).astype(BF)

    for p in range(6):
        target = targets(ids_ref[p // 2, p % 2, 0])
        ptab[p] = (code_rows == target).astype(F32).astype(BF)
        pttab[p] = way_back(target)
        gate = jnp.sum(jnp.where(eye, gates_ref[p // 2, p % 2, 0], 0.0), axis=1, keepdims=True)
        gtab[p] = jnp.broadcast_to(gate, (TOK, 128))

    mirror_sources = [right_cot.at[0], right_saved.at[0, 0], right_in.at[0], right_saved.at[1, 0]]
    id_swap = remote(ids_ref, partner_ids, id_sem.at[0], id_sem.at[1], sec, partner)
    mirrors = [
        remote(src, mir.at[i], mir_sem.at[0, i], mir_sem.at[1, i], mirror, me)
        for i, src in enumerate(mirror_sources)
    ]

    quarter64 = iota((TOK, CHUNK), 0) % 4
    quarter128 = iota((128, CHUNK), 0) % 4

    def gather(unit, p, read, scaled):
        place = ptab[p]
        extra = None
        for c in range(4):
            cols = pl.ds(c * CHUNK, CHUNK)
            block = read(cols)
            if scaled:
                block = (gtab[p][:, 0:1] * block.astype(F32)).astype(BF)
            routed = dot(place, block)
            send[unit, :, :, cols] = routed[:64].reshape(8, 8, CHUNK).astype(BF)
            tail = routed[64:]
            extra = tail if c == 0 else jnp.where(quarter64 == c, tail, extra)
        send[unit, :, :, pl.ds(D, CHUNK)] = extra.reshape(8, 8, CHUNK).astype(BF)
        recv[unit, x] = send[unit, mine]

    def ship(unit):
        for dest, a, _, expert in peers:
            remote(
                send.at[unit, expert],
                recv.at[unit, 4 * a + x],
                s1_send.at[unit],
                s1_recv.at[unit, a],
                sec,
                dest,
            ).start()

    def relay(unit):
        for a in (1, 0):
            count = 4 if a else 3
            span = recv.at[unit, pl.ds(4 * a, count)]
            remote(span, span, s1_send.at[unit], s1_recv.at[unit, a], sec, partner).wait_recv()
            remote(
                recv.at[unit, pl.ds(4 * a, 4)],
                recv.at[unit, pl.ds(8 + 4 * a, 4)],
                rl_send.at[unit, a],
                rl_recv.at[unit, a],
                sec,
                partner,
            ).start()

    def relayed(unit):
        for a in (1, 0):
            span = recv.at[unit, pl.ds(4 * a, 4)]
            remote(span, span, rl_send.at[unit, a], rl_recv.at[unit, a], sec, partner).wait_recv()

    pick_j = iota((32, 128), 1)
    pick_r = iota((32, 128), 0)
    spread = (lax.div(iota((128, 32), 0), 4) == iota((128, 32), 1)).astype(F32).astype(BF)

    def unfold(unit, dst, base):
        for c in range(4):
            cols = pl.ds(c * CHUNK, CHUNK)
            first = recv[unit, :, :, cols].astype(F32).reshape(128, CHUNK).astype(BF)
            dst[pl.ds(base, 128), cols] = first
        tail = recv[unit, :, :, pl.ds(D, CHUNK)].astype(F32).reshape(128, CHUNK).astype(BF)
        for c in range(4):
            pick = (pick_j == 4 * pick_r + c).astype(F32).astype(BF)
            dst[pl.ds(base + 128, 32), pl.ds(c * CHUNK, CHUNK)] = dot(pick, tail).astype(BF)

    def fold(r, chunk_of):
        extra = None
        for c in range(4):
            rows = chunk_of(c)
            part[r, :, :, pl.ds(c * CHUNK, CHUNK)] = (
                rows[:128].reshape(16, 8, CHUNK).astype(BF)
            )
            tail = dot(spread, rows[128:].astype(BF))
            extra = tail if c == 0 else jnp.where(quarter128 == c, tail, extra)
        part[r, :, :, pl.ds(D, CHUNK)] = extra.reshape(16, 8, CHUNK).astype(BF)

    def hand_over(r):
        for a in (1, 0):
            remote(
                part.at[r, pl.ds(8 + 4 * a, 4)],
                half.at[r, pl.ds(4 * a, 4)],
                pt_send.at[r, a],
                pt_recv.at[r, a],
                sec,
                partner,
            ).start()

    def hand_out(r):
        for dest, a, xd, _ in peers:
            remote(
                part.at[r, 8 + 4 * a + xd],
                half.at[r, mine],
                pt_send.at[r, 0],
                pt_recv.at[r, 0],
                sec,
                dest,
            ).start()
        for dest, a, xd, _ in peers:
            remote(
                part.at[r, 4 * a + xd],
                vals.at[r, mine],
                sm_send.at[r],
                sm_recv.at[r],
                sec,
                dest,
            ).start()
        half[r, mine] = part[r, 8 + x]
        vals[r, mine] = part[r, x]

    def gate_up(rows):
        return [dot(rows[...], wgu[:, pl.ds(256 * i, 256)]) for i in range(3)]

    def expert_forward(unit, r, give):
        relayed(unit)
        unfold(unit, xfwd, 0)
        both = jnp.concatenate(gate_up(xfwd), axis=1)
        gate, up = both[:, :HALF], both[:, HALF:]
        hidden = (gate * jax.nn.sigmoid(gate) * up).astype(BF)
        fold(r, lambda c: dot(hidden, wd[:, pl.ds(c * CHUNK, CHUNK)]))
        give(r)

    def backward_inputs(unit_x, index):
        base = index * ROWS
        rows = pl.ds(base, ROWS)
        relayed(unit_x)
        unfold(unit_x, xall, base)
        both = jnp.concatenate(gate_up(xall.at[rows]), axis=1)
        gate, up = both[:, :HALF], both[:, HALF:]
        logistic = jax.nn.sigmoid(gate)
        swish = gate * logistic
        hid[rows] = (swish * up).astype(BF)
        return gate, up, logistic, swish

    def backward_rest(unit_c, index, r, kept):
        gate, up, logistic, swish = kept
        base = index * ROWS
        rows = pl.ds(base, ROWS)
        relayed(unit_c)
        unfold(unit_c, call, base)
        d_hidden = dot_nt(call[rows], wd[...])
        d_gate = (d_hidden * up * logistic * (1.0 + gate * (1.0 - logistic))).astype(BF)
        d_up = (d_hidden * swish).astype(BF)
        dgu[rows, pl.ds(0, HALF)] = d_gate
        dgu[rows, pl.ds(HALF, HALF)] = d_up
        fold(r, lambda c: dot_nt(dgu[rows], wgu[pl.ds(c * CHUNK, CHUNK), :]))
        hand_over(r)

    def expert_backward(unit_x, unit_c, index, r):
        backward_rest(unit_c, index, r, backward_inputs(unit_x, index))

    def add_halves(r):
        for a in (1, 0):
            span = half.at[r, pl.ds(4 * a, 4)]
            remote(span, span, pt_send.at[r, a], pt_recv.at[r, a], sec, partner).wait_recv()
            for i in range(4 * a, 4 * a + 4):
                sums[r, i] = (part[r, i].astype(F32) + half[r, i].astype(F32)).astype(BF)
            for dest, side, xd, _ in peers:
                if side == a:
                    remote(
                        sums.at[r, 4 * a + xd],
                        vals.at[r, mine],
                        sm_send.at[r],
                        sm_recv.at[r],
                        sec,
                        dest,
                    ).start()
        vals[r, mine] = sums[r, x]

    def rows_back(slabs, back, c):
        first = slabs[:, :, pl.ds(c * CHUNK, CHUNK)].astype(F32).reshape(TOK, CHUNK)
        tail = slabs[:, :, pl.ds(D, CHUNK)].astype(F32).reshape(TOK, CHUNK)
        last = jnp.where(quarter64 == c, tail, 0.0)
        return dot(back, jnp.concatenate([first, last], axis=0).astype(BF))

    def arrived(r):
        span = vals.at[r, pl.ds(0, 7)]
        remote(span, span, sm_send.at[r], sm_recv.at[r], sec, partner).wait_recv()

    def combine(r, p, read, scaled, index):
        arrived(r)
        for c in range(4):
            cols = pl.ds(c * CHUNK, CHUNK)
            got = rows_back(vals.at[r], pttab[p], c)
            if scaled:
                got = gtab[p][:, 0:1] * got
            outs[index, :, cols] = (read(cols).astype(F32) + got).astype(BF)

    swap = remote(gathered, swapped, gt_sem.at[0], gt_sem.at[1], sec, partner)

    def swap_parts(r, p):
        id_swap.wait_recv()
        back = way_back(targets(partner_ids[p // 2, p % 2, 0]))
        span = half.at[r, pl.ds(0, 7)]
        remote(span, span, pt_send.at[r, 0], pt_recv.at[r, 0], sec, partner).wait_recv()
        for c in range(4):
            gathered[:, pl.ds(c * CHUNK, CHUNK)] = rows_back(half.at[r], back, c).astype(BF)
        swap.start()

    def combine_swapped(r, p, read, index):
        arrived(r)
        swap.wait_recv()
        for c in range(4):
            cols = pl.ds(c * CHUNK, CHUNK)
            both = rows_back(vals.at[r], pttab[p], c) + swapped[:, cols].astype(F32)
            got = gtab[p][:, 0:1] * both.astype(BF).astype(F32)
            outs[index, :, cols] = (read(cols).astype(F32) + got).astype(BF)

    def from_tok(i):
        return lambda cols: tok[i, :, cols]

    def from_mir(i):
        return lambda cols: mir[i, :, cols]

    def choose(edge, i, j):
        return lambda cols: jnp.where(
            sec == edge, tok[i, :, cols].astype(F32), passed[j, :, cols].astype(F32)
        ).astype(BF)

    left_two = choose(0, 3, 0)
    cot_two = choose(15, 4, 1)
    pass_left = remote(outs.at[0], passed.at[0], ps_sem.at[0, 0], ps_sem.at[1, 0], after, me)
    pass_right = remote(outs.at[1], passed.at[1], ps_sem.at[0, 1], ps_sem.at[1, 1], ahead, me)
    def grads_of_inputs(i, carry):
        cols = pl.ds(pl.multiple_of(i * 256, 256), 256)
        total = dot_tn(xall[:, cols], dgu[...]).astype(BF)
        gg_buf[cols, :] = total[:, :HALF]
        gu_buf[cols, :] = total[:, HALF:]
        return carry

    def grads_of_down(i, carry):
        cols = pl.ds(pl.multiple_of(i * 256, 256), 256)
        gd_buf[:, cols] = dot_tn(hid[...], call[:, cols]).astype(BF)
        return carry

    R_F0, R_B0, R_F1, R_B1, R_F2, R_B2 = range(6)
    loads[0].wait()
    gather(U_F0, F0, from_tok(0), False)
    loads[1].wait()
    gather(U_B1X, B1, from_tok(1), False)
    loads[2].wait()
    gather(U_B1C, B1, from_tok(2), True)

    pl.semaphore_wait(barrier, 11)
    for i in (1, 0, 2, 3):
        mirrors[i].start()
    id_swap.start()
    ship(U_B1X)
    ship(U_B1C)
    relay(U_B1X)
    ship(U_F0)
    relay(U_F0)
    relay(U_B1C)
    for copy in loads[3:]:
        copy.wait()
    expert_forward(U_F0, R_F0, hand_over)
    mirrors[1].wait_recv()
    gather(U_B0X, B0, from_mir(1), False)
    ship(U_B0X)
    relay(U_B0X)
    mirrors[0].wait_recv()
    gather(U_B0C, B0, from_mir(0), True)
    ship(U_B0C)
    relay(U_B0C)
    add_halves(R_F0)
    expert_backward(U_B1X, U_B1C, 0, R_B1)
    combine(R_F0, F0, from_tok(0), True, 0)
    pass_left.start()
    pass_left.wait_recv()
    gather(U_F2, F2, left_two, False)
    ship(U_F2)
    relay(U_F2)
    mirrors[2].wait_recv()
    add_halves(R_B1)
    gather(U_F1, F1, from_mir(2), False)
    ship(U_F1)
    mirrors[3].wait_recv()
    expert_backward(U_B0X, U_B0C, 1, R_B0)
    gather(U_B2X, B2, from_mir(3), False)
    ship(U_B2X)
    combine(R_B1, B1, from_tok(2), False, 3)
    relay(U_F1)
    expert_forward(U_F2, R_F2, hand_over)
    add_halves(R_B0)
    combine(R_B0, B0, from_mir(0), False, 1)
    pass_right.start()
    pass_right.wait_recv()
    gather(U_B2C, B2, cot_two, True)
    ship(U_B2C)
    relay(U_B2X)
    expert_forward(U_F1, R_F1, hand_out)
    relay(U_B2C)
    swap_parts(R_F1, F1)
    kept = backward_inputs(U_B2X, 2)
    add_halves(R_F2)
    combine(R_F2, F2, left_two, True, 4)
    backward_rest(U_B2C, 2, R_B2, kept)
    lax.fori_loop(0, 8, grads_of_inputs, 0)
    add_halves(R_B2)
    lax.fori_loop(0, 8, grads_of_down, 0)
    combine_swapped(R_F1, F1, from_mir(2), 2)
    combine(R_B2, B2, cot_two, False, 5)

    for copy in mirrors:
        copy.wait_send()
    id_swap.wait_send()
    swap.wait_send()
    pass_left.wait_send()
    pass_right.wait_send()
    for unit in range(9):
        span = send.at[unit, pl.ds(0, 7)]
        remote(span, span, s1_send.at[unit], s1_recv.at[unit, 0], sec, partner).wait_send()
        for a in range(2):
            span = recv.at[unit, pl.ds(4 * a, 4)]
            remote(span, span, rl_send.at[unit, a], rl_recv.at[unit, a], sec, partner).wait_send()
    for r in range(6):
        for a in range(1 if r == R_F1 else 2):
            span = part.at[r, pl.ds(8, 7 if r == R_F1 else 4)]
            remote(span, span, pt_send.at[r, a], pt_recv.at[r, a], sec, partner).wait_send()
        span = sums.at[r, pl.ds(0, 7)]
        remote(span, span, sm_send.at[r], sm_recv.at[r], sec, partner).wait_send()


def write_out(
    outs,
    gg_buf,
    gu_buf,
    gd_buf,
    left_out,
    right_out,
    left_back,
    right_back,
    grad_gate,
    grad_up,
    grad_down,
    sem,
):
    pairs = []
    for src, dst in ((gg_buf, grad_gate), (gu_buf, grad_up), (gd_buf, grad_down)):
        count = src.shape[0] // 4
        for i in range(4):
            pairs.append((src.at[pl.ds(i * count, count)], dst.at[pl.ds(i * count, count)]))
    pairs += [
        (outs.at[0], left_out.at[0]),
        (outs.at[1], right_back.at[0]),
        (outs.at[2], right_out),
        (outs.at[3], left_back),
        (outs.at[4], left_out.at[1]),
        (outs.at[5], right_back.at[1]),
    ]
    copies = [pltpu.make_async_copy(a, b, sem.at[i]) for i, (a, b) in enumerate(pairs)]
    for copy in copies:
        copy.start()
    for copy in copies:
        copy.wait()


def per_device(
    left_in,
    left_new,
    left_saved,
    left_cot,
    right_in,
    right_saved,
    right_cot,
    right_cot_new,
    expert_ids,
    gate_values,
    w_gate,
    w_up,
    w_down,
):
    ids = jnp.swapaxes(expert_ids, 3, 4)
    gates = jnp.swapaxes(gate_values, 3, 4)
    hbm = pl.BlockSpec(memory_space=pltpu.HBM)
    vmem = pl.BlockSpec(memory_space=pltpu.VMEM)
    sds = jax.ShapeDtypeStruct
    dma = pltpu.SemaphoreType.DMA
    results = pl.pallas_call(
        kernel,
        name="relay",
        out_shape=(
            pltpu.VMEM((6, TOK, D), BF),
            pltpu.VMEM((D, HALF), BF),
            pltpu.VMEM((D, HALF), BF),
            pltpu.VMEM((HALF, D), BF),
        ),
        in_specs=[hbm] * 13,
        out_specs=(vmem,) * 4,
        scratch_shapes=[
            pltpu.VMEM((3, 2, 1, 1, TOK), jnp.int32),
            pltpu.VMEM((3, 2, 1, 1, TOK), F32),
            pltpu.VMEM((3, 2, 1, 1, TOK), jnp.int32),
            pltpu.VMEM((TOK, D), BF),
            pltpu.VMEM((TOK, D), BF),
            pltpu.VMEM((6, 128, TOK), BF),
            pltpu.VMEM((6, TOK, 128), BF),
            pltpu.VMEM((6, TOK, 128), F32),
            pltpu.VMEM((D, 2 * HALF), BF),
            pltpu.VMEM((HALF, D), BF),
            pltpu.VMEM((5, TOK, D), BF),
            pltpu.VMEM((4, TOK, D), BF),
            pltpu.VMEM((2, TOK, D), BF),
            pltpu.VMEM((9, 8, 8, SLAB), BF),
            pltpu.VMEM((9, 16, 8, SLAB), BF),
            pltpu.VMEM((6, 16, 8, SLAB), BF),
            pltpu.VMEM((6, 8, 8, SLAB), BF),
            pltpu.VMEM((6, 8, 8, SLAB), BF),
            pltpu.VMEM((6, 8, 8, SLAB), BF),
            pltpu.VMEM((3 * ROWS, D), BF),
            pltpu.VMEM((3 * ROWS, D), BF),
            pltpu.VMEM((3 * ROWS, 2 * HALF), BF),
            pltpu.VMEM((3 * ROWS, HALF), BF),
            pltpu.VMEM((ROWS, D), BF),
            dma((10,)),
            dma((2, 4)),
            dma((9,)),
            dma((9, 2)),
            dma((9, 2)),
            dma((9, 2)),
            dma((6, 2)),
            dma((6, 2)),
            dma((6,)),
            dma((6,)),
            dma((2, 2)),
            dma((2,)),
            dma((2,)),
        ],
        compiler_params=pltpu.CompilerParams(
            collective_id=0, has_side_effects=True, vmem_limit_bytes=60700000
        ),
    )(
        ids,
        gates,
        left_in,
        left_new,
        left_saved,
        left_cot,
        right_in,
        right_saved,
        right_cot,
        right_cot_new,
        w_gate,
        w_up,
        w_down,
    )
    left_out, right_out, left_back, right_back, gg, gu, gd = pl.pallas_call(
        write_out,
        name="write_out",
        out_shape=(
            sds((2, TOK, D), BF),
            sds((TOK, D), BF),
            sds((TOK, D), BF),
            sds((2, TOK, D), BF),
            sds((D, HALF), BF),
            sds((D, HALF), BF),
            sds((HALF, D), BF),
        ),
        in_specs=[vmem] * 4,
        out_specs=(hbm,) * 7,
        scratch_shapes=[dma((18,))],
        compiler_params=pltpu.CompilerParams(vmem_limit_bytes=4 * 1024 * 1024),
    )(*results)
    return (
        left_out[:, None],
        right_out[None],
        left_back[None],
        right_back[:, None],
        gg[None, None],
        gu[None, None],
        gd[None, None],
    )


def solution(mesh):
    in_specs = (
        P("section", "expert", None),
        P("expert", None),
        P("section", "expert", None),
        P("section", "expert", None),
        P("section", "expert", None),
        P(None, "section", "expert", None),
        P("section", "expert", None),
        P("expert", None),
        P(None, None, "section", "expert", None),
        P(None, None, "section", "expert", None),
        P("section", "expert", None, None),
        P("section", "expert", None, None),
        P("section", "expert", None, None),
    )
    out_specs = (
        P(None, "section", "expert", None),
        P("section", "expert", None),
        P("section", "expert", None),
        P(None, "section", "expert", None),
        P("section", "expert", None, None),
        P("section", "expert", None, None),
        P("section", "expert", None, None),
    )
    return jax.shard_map(
        per_device, mesh=mesh, in_specs=in_specs, out_specs=out_specs, check_vma=False
    )
```
